128 devices in a mesh: path: 8 (over y, core), fsdp: 16 (over z, x).
Axes of the slice: x: 4, y: 4, z: 4, core: 2. Of those that a mesh axis runs over, the one named last changes fastest.
Arguments:
- input_activation_matrix: bfloat16 [8, 3072, 2048], P('path', 'fsdp'), may hold values from -6 to 6
- output_sensitivity: bfloat16 [8, 3072, 2048], P('path', 'fsdp'), may hold values from -12 to 12
- trajectory_initial_parameters: bfloat16 [8, 8, 1024, 4096], P('path', None, 'fsdp'), may hold values from -6 to 6
- trajectory_gradient_average: bfloat16 [8, 8, 1024, 4096], P('path', None, 'fsdp'), may hold values from -0.19921875 to 0.19921875
- trajectory_squared_average: bfloat16 [8, 8, 1024, 4096], P('path', None, 'fsdp'), may hold values from 0.0009994507 to 0.099609375
- common_expert_parameters: float32 [8, 2, 1024, 4096], P('path', None, 'fsdp'), may hold values from -6 to 6
- outer_inertia: float32 [8, 2, 1024, 4096], P('path', None, 'fsdp'), may hold values from -0.4 to 0.4
- trajectory_membership: int32 [8, 8], replicated, may hold values from 0 to 1
- punctual_flags: int32 [8], replicated, may hold values 0 or 1
Outputs:
- refreshed_experts: float32 [8, 2, 1024, 4096], P('path', None, 'fsdp')
- refreshed_inertia: float32 [8, 2, 1024, 4096], P('path', None, 'fsdp')
- returned: bfloat16 [8, 8, 1024, 4096], P('path', None, 'fsdp')
The draws below stay inside these ranges and needn't reach their ends.
All inputs are finite; a program needn't handle non-finite values.
Results may differ from the reference program's by a relative error of at most 0.0024.
Values may be sent and summed in bfloat16 or wider, within the bound.
No kernel may reach another device: no remote copies, remote signals or barrier semaphores. Data moves between devices by JAX's collectives and lax.ppermute only.
A program may use at most 320 MiB of HBM per device.

```python
import math
import jax
import jax.numpy as jnp
from jax import lax

D = 2048
UNIT = 1024
SETS = 8
MPS = 2
STEP = 1000
TRAJECTORY_SUM = 8
TOKP = 3072


def touch_ends(array, own_key, smallest, largest):
    longest = array.shape.index(max(array.shape))
    spots = []
    for shift in (0, 1):
        where = [jax.random.randint(jax.random.fold_in(own_key, axis), (), 0, length) for axis, length in enumerate(array.shape)]
        where[longest] = (where[longest] + shift) % array.shape[longest]
        spots.append(tuple(where))
    return array.at[spots[0]].set(smallest).at[spots[1]].set(largest)


def block_levels(own_key, shape, pieces, smallest, largest):
    level = 1.0
    for position, parts in pieces:
        draws = jax.random.uniform(jax.random.fold_in(jax.random.fold_in(own_key, 6), position), (parts,), jnp.float32, smallest / len(pieces), largest / len(pieces))
        level = level * jnp.repeat(jnp.exp(draws), shape[position] // parts).reshape((-1,) + (1,) * (len(shape) - 1 - position))
    return level


def noise(key, shape, width, bound, shards=(), kind=jnp.bfloat16):
    level = block_levels(key, shape, shards, -0.22, 0.18) if shards else 1.0
    drawn = jax.random.normal(key, shape, jnp.float32) * width * level
    return jnp.minimum(jnp.maximum(drawn, -bound), bound).astype(kind)


def setup_inputs(seed: int = 0) -> dict:
    splits = jax.random.split(jax.random.key(seed), 10)
    input_activation_matrix = noise(splits[0], (TRAJECTORY_SUM, TOKP, D), 1.0, 6.0, ((0, 8), (1, 16)))
    output_sensitivity = noise(splits[1], (TRAJECTORY_SUM, TOKP, D), 2.0, 12.0, ((0, 8), (1, 16)))
    trajectory_initial_parameters = noise(splits[2], (TRAJECTORY_SUM, SETS, UNIT, 2 * D), 1.0, 6.0, ((0, 8), (2, 16)))
    trajectory_gradient_average = noise(splits[3], (TRAJECTORY_SUM, SETS, UNIT, 2 * D), 0.03, 0.19921875, ((0, 8), (2, 16)))
    trajectory_squared_average = jnp.clip(jnp.exp(math.log(0.099609375) - 4.6018058 * jax.random.uniform(splits[4], (TRAJECTORY_SUM, SETS, UNIT, 2 * D), jnp.float32) ** block_levels(splits[4], (TRAJECTORY_SUM, SETS, UNIT, 2 * D), ((0, 8), (2, 16)), -0.2, 0.2)), 0.0009994507, 0.099609375).astype(jnp.bfloat16)
    common_expert_parameters = noise(splits[5], (SETS, MPS, UNIT, 2 * D), 1.0, 6.0, ((0, 8), (2, 16)), jnp.float32)
    outer_inertia = noise(splits[6], (SETS, MPS, UNIT, 2 * D), 0.05, 0.4, ((0, 8), (2, 16)), jnp.float32)
    trajectory_membership = touch_ends(jax.random.randint(splits[7], (TRAJECTORY_SUM, SETS), 0, MPS), jax.random.fold_in(splits[7], 1), 0, MPS - 1).astype(jnp.int32)
    punctual_flags = touch_ends((jax.random.randint(splits[8], (TRAJECTORY_SUM,), 0, 2) < 1).astype(jnp.int32), jax.random.fold_in(splits[8], 1), 0, 1)
    return {"input_activation_matrix": input_activation_matrix, "output_sensitivity": output_sensitivity, "trajectory_initial_parameters": trajectory_initial_parameters, "trajectory_gradient_average": trajectory_gradient_average, "trajectory_squared_average": trajectory_squared_average, "common_expert_parameters": common_expert_parameters, "outer_inertia": outer_inertia, "trajectory_membership": trajectory_membership, "punctual_flags": punctual_flags}


BETA_ONE = 0.9
BETA_TWO = 0.999
ADAM_EPS = 1e-08
INNER_RATE = 0.05
DECAY = 0.1
GLOBAL_LEARNING = 0.7
INERTIA_FACTOR = 0.9

def adam_delta(grads, first, second, start):
    corr_one = 1.0 - BETA_ONE ** STEP
    corr_two = 1.0 - BETA_TWO ** STEP
    first_new = BETA_ONE * first.astype(jnp.float32) + (1.0 - BETA_ONE) * grads
    second_new = BETA_TWO * second.astype(jnp.float32) + (1.0 - BETA_TWO) * grads * grads
    direction = first_new / corr_one / (jnp.sqrt(second_new / corr_two) + ADAM_EPS)
    return (INNER_RATE * (direction + DECAY * start.astype(jnp.float32))).astype(jnp.bfloat16)

def path_grads(unit_rows, inputs, upstream):
    features = inputs.shape[1]
    in_rows = unit_rows[:, :features]
    out_rows = unit_rows[:, features:]
    input_scale = features ** (-0.5)
    hidden_scale = (SETS * UNIT) ** (-0.5)
    preact = jnp.dot(inputs, in_rows.T, preferred_element_type=jnp.float32) * input_scale
    active, pullback = jax.vjp(jax.nn.gelu, preact)
    active_half = active.astype(jnp.bfloat16)
    back_active = jnp.dot(upstream, out_rows.T, preferred_element_type=jnp.float32) * hidden_scale
    back_preact = pullback(back_active)[0].astype(jnp.bfloat16)
    grad_in = jnp.dot(back_preact.T, inputs, preferred_element_type=jnp.float32) * input_scale
    grad_out = jnp.dot(active_half.T, upstream, preferred_element_type=jnp.float32) * hidden_scale
    return jnp.concatenate([grad_in, grad_out], axis=1)

def reference(input_activation_matrix, output_sensitivity, trajectory_initial_parameters, trajectory_gradient_average, trajectory_squared_average, common_expert_parameters, outer_inertia, trajectory_membership, punctual_flags):
    eligible_trajectories = jnp.arange(MPS, dtype=jnp.int32)
    picked_trajectories = jnp.where((trajectory_membership[:, :, None] == eligible_trajectories[None, None, :]) & (punctual_flags[:, None, None] == 1), 1.0, 0.0).astype(jnp.float32)

    def accumulate(aggregate_change, items):
        inputs, upstream, start, first, second, weights = items
        unit_rows = start.reshape(SETS * UNIT, 2 * D)
        grads = path_grads(unit_rows, inputs, upstream)
        pseudo = adam_delta(grads, first.reshape(SETS * UNIT, 2 * D), second.reshape(SETS * UNIT, 2 * D), unit_rows)
        pseudo = pseudo.reshape(SETS, UNIT, 2 * D)
        return (aggregate_change + weights[:, :, None, None] * pseudo.astype(jnp.float32)[:, None], None)
    initial = jnp.zeros((SETS, MPS, UNIT, 2 * D), jnp.float32)
    aggregate_change, _ = lax.scan(accumulate, initial, (input_activation_matrix, output_sensitivity, trajectory_initial_parameters, trajectory_gradient_average, trajectory_squared_average, picked_trajectories))
    punctual_tally = lax.optimization_barrier(jnp.sum(picked_trajectories, axis=0))
    punctual_average = aggregate_change / jnp.maximum(punctual_tally, 1.0)[:, :, None, None]
    refreshed_inertia = INERTIA_FACTOR * outer_inertia + punctual_average
    refreshed_experts = common_expert_parameters - GLOBAL_LEARNING * (punctual_average + INERTIA_FACTOR * refreshed_inertia)
    updated = refreshed_experts.astype(jnp.bfloat16)
    set_index = jnp.arange(SETS, dtype=jnp.int32)
    returned = updated[set_index[None, :], trajectory_membership]
    return (refreshed_experts, refreshed_inertia, returned)
```

```python
import functools

import jax
import jax.numpy as jnp
from jax import lax
from jax.experimental import pallas as pl
from jax.experimental.pallas import tpu as pltpu
from jax.sharding import PartitionSpec as P

UNIT = 1024
SETS = 8
STEP = 1000


BETA_ONE = 0.9
BETA_TWO = 0.999
ADAM_EPS = 1e-08
INNER_RATE = 0.05
DECAY = 0.1
GLOBAL_LEARNING = 0.7
INERTIA_FACTOR = 0.9

ZS, XS, YS = 4, 4, 4
GELU_C = 0.7978845608028654
GELU_A = 0.044715
NT = (((1,), (1,)), ((), ()))
F32 = jnp.float32
BF16 = jnp.bfloat16
COLS = 512
CHUNK = 384


def plane_hop(da, db):
    pairs = []
    for p in range(2 * YS):
        dz, dx = (da, db) if p % 2 == 0 else (db, da)
        for z in range(ZS):
            for x in range(XS):
                to = ((z + dz) % ZS) * XS + (x + dx) % XS
                pairs.append((p * ZS * XS + z * XS + x, p * ZS * XS + to))
    return pairs


def path_hop(hop, flip):
    return [
        (i, ((i // 2 + (hop if i % 2 == 0 else -hop)) % YS) * 2 + ((i % 2) ^ flip))
        for i in range(2 * YS)
    ]


def on_path(a, hop, flip=0):
    return lax.ppermute(a, "path", path_hop(hop, flip))


def after(a, *others):
    return lax.optimization_barrier((a, *others))[0]


def gather_tokens(x, g, compute):
    last = {}
    hold = []

    def send(a, da, db):
        nonlocal hold
        others = hold + ([last[da, db]] if (da, db) in last else [])
        if others:
            a = after(a, *others)
        out = lax.ppermute(a, ("path", "fsdp"), plane_hop(da, db))
        last[da, db] = out
        return out

    half = x.shape[0] // 2
    xb, gb = {(0, 0): x}, {(0, 0): g}
    xb[0, -1], xb[0, 1] = send(x, 0, 1), send(x, 0, -1)
    gb[-1, 0], gb[1, 0] = send(g, 1, 0), send(g, -1, 0)
    xt, xl = send(xb[0, -1][:half], 0, 1), send(xb[0, 1][half:], 0, -1)
    gt, gl = send(gb[-1, 0][:half], 1, 0), send(gb[1, 0][half:], -1, 0)
    xb[0, 2] = jnp.concatenate([xt, xl], 0)
    gb[2, 0] = jnp.concatenate([gt, gl], 0)
    ups = [(-1, 0), (-1, -1), (-1, 1), (-1, 2), (2, 2), (2, 1)]
    downs = [(1, 0), (1, -1), (1, 1), (2, 0), (2, -1), (1, 2)]
    for r in range(6):
        a, b = ups[r]
        c, d = downs[r]
        new = (
            send(xb[0 if a == -1 else -1, b], 1, 0),
            send(xb[0 if c == 1 else 1, d], -1, 0),
            send(gb[b, 0 if a == -1 else -1], 0, 1),
            send(gb[d, 0 if c == 1 else 1], 0, -1),
        )
        xb[a, b], xb[c, d], gb[b, a], gb[d, c] = new
        hold = [t for t in (compute(r, xb, gb),) if t is not None]
    return xb, gb


def hidden_both(xs, gs, w, act_t, dpre_t, features, hidden_scale):
    in_scale = features ** (-0.5)

    def chunk(t, carry):
        rows = pl.ds(pl.multiple_of(t * CHUNK, CHUNK), CHUNK)
        pre = (
            lax.dot_general(w[:, :features], xs[rows, :], NT, preferred_element_type=F32)
            * in_scale
        )
        back = (
            lax.dot_general(w[:, features:], gs[rows, :], NT, preferred_element_type=F32)
            * hidden_scale
        )
        sq = pre * pre
        t_ = jnp.tanh(GELU_C * pre * (1.0 + GELU_A * sq))
        cdf = 0.5 * (1.0 + t_)
        slope = cdf + (0.5 * GELU_C) * pre * (1.0 - t_ * t_) * (1.0 + (3.0 * GELU_A) * sq)
        act_t[:, rows] = (pre * cdf).astype(BF16)
        dpre_t[:, rows] = (back * slope).astype(BF16)
        return carry

    lax.fori_loop(0, xs.shape[0] // CHUNK, chunk, 0)


def stage(pieces, dst, sem):
    copies, at = [], 0
    for p in pieces:
        copies.append(pltpu.make_async_copy(p, dst.at[pl.ds(at, p.shape[0]), :], sem.at[len(copies)]))
        at += p.shape[0]
    return copies


def grads_kernel(n, first, features, hidden_scale, *refs):
    refs = list(refs)
    x_refs, g_refs, w_ref = refs[:n], refs[n : 2 * n], refs[2 * n]
    at = 2 * n + 1
    acc = None
    if not first:
        acc = refs[at]
        at += 1
    out, xs, gs, w, act_t, dpre_t, xsem, gsem, wsem = refs[at:]
    i = pl.program_id(0)
    half = pl.num_programs(0) // 2

    @pl.when(i == 0)
    def _():
        copies = stage(x_refs, xs, xsem) + stage(g_refs, gs, gsem)
        copies.append(pltpu.make_async_copy(w_ref, w, wsem))
        for c in copies:
            c.start()
        for c in copies:
            c.wait()
        hidden_both(xs, gs, w, act_t, dpre_t, features, hidden_scale)

    def add(term):
        out[...] = term if first else acc[...] + term

    @pl.when(i < half)
    def _():
        cols = pl.ds(pl.multiple_of(i * COLS, COLS), COLS)
        add(jnp.dot(dpre_t[...], xs[:, cols], preferred_element_type=F32))

    @pl.when(i >= half)
    def _():
        cols = pl.ds(pl.multiple_of((i - half) * COLS, COLS), COLS)
        add(jnp.dot(act_t[...], gs[:, cols], preferred_element_type=F32))


ANY = pl.BlockSpec(memory_space=pl.ANY)


def accumulate(xp, gp, w, acc, hidden_scale):
    n = len(xp)
    units, width = w.shape
    features = width // 2
    tokens = sum(p.shape[0] for p in xp)
    first = acc is None
    block = pl.BlockSpec((units, COLS), lambda i: (0, i))
    flops = 8 * tokens * units * features
    return pl.pallas_call(
        functools.partial(grads_kernel, n, first, features, hidden_scale),
        grid=(width // COLS,),
        in_specs=[ANY] * (2 * n + 1) + ([] if first else [block]),
        out_specs=block,
        out_shape=jax.ShapeDtypeStruct((units, width), F32),
        scratch_shapes=[
            pltpu.VMEM((tokens, features), BF16),
            pltpu.VMEM((tokens, features), BF16),
            pltpu.VMEM((units, width), BF16),
            pltpu.VMEM((units, tokens), BF16),
            pltpu.VMEM((units, tokens), BF16),
            pltpu.SemaphoreType.DMA((n,)),
            pltpu.SemaphoreType.DMA((n,)),
            pltpu.SemaphoreType.DMA,
        ],
        input_output_aliases={} if first else {2 * n + 1: 0},
        compiler_params=pltpu.CompilerParams(vmem_limit_bytes=58 << 20),
        cost_estimate=pl.CostEstimate(
            flops=flops,
            bytes_accessed=units * width * (2 + 8) + tokens * width * 2,
            transcendentals=units * tokens,
        ),
        name="grads",
    )(*xp, *gp, w, *(() if first else (acc,)))


def adam(total, scale, first, second, start):
    corr_one = 1.0 - BETA_ONE**STEP
    corr_two = 1.0 - BETA_TWO**STEP
    raw = total * scale
    first_new = (INNER_RATE * BETA_ONE / corr_one) * first.astype(F32) + (
        INNER_RATE * (1.0 - BETA_ONE) / corr_one
    ) * raw
    second_new = (BETA_TWO / corr_two) * second.astype(F32) + (
        (1.0 - BETA_TWO) / corr_two
    ) * (raw * raw)
    root = second_new * lax.rsqrt(second_new)
    return (first_new / (root + ADAM_EPS) + (INNER_RATE * DECAY) * start.astype(F32)).astype(BF16)


def pseudo_kernel(n, lead, features, hidden_scale, *refs):
    refs = list(refs)
    where = refs[0]
    at = 1
    if lead:
        x_refs, g_refs, w_ref = refs[at : at + n], refs[at + n : at + 2 * n], refs[at + 2 * n]
        at += 2 * n + 1
    else:
        g_refs, act_ref = refs[at : at + n], refs[at + n]
        at += n + 1
    acc, m_ref, v_ref, r_ref = refs[at : at + 4]
    at += 4
    if lead:
        keep, swap, act_out, total, xs, gs, w, act_t, dpre_t, xsem, gsem, wsem, asem = refs[at:]
    else:
        keep, swap, total, xs, dpre_t, xsem, asem = refs[at:]
    i = pl.program_id(0)

    @pl.when(i == 0)
    def _():
        if lead:
            copies = stage(x_refs, xs, xsem) + stage(g_refs, gs, gsem)
            copies.append(pltpu.make_async_copy(w_ref, w, wsem))
        else:
            copies = stage(g_refs, xs, xsem)
            copies.append(pltpu.make_async_copy(act_ref, dpre_t, asem))
        for c in copies:
            c.start()
        for c in copies:
            c.wait()
        if lead:
            hidden_both(xs, gs, w, act_t, dpre_t, features, hidden_scale)
            pltpu.make_async_copy(act_t, act_out, asem).start()

    scale = features ** (-0.5) if lead else hidden_scale
    cols = pl.ds(pl.multiple_of(i * COLS, COLS), COLS)
    total[...] = acc[...] + jnp.dot(dpre_t[...], xs[:, cols], preferred_element_type=F32)
    y, core = where[0], where[1]
    rows = acc.shape[0] // SETS
    for d in range(YS):
        for out, parity in ((keep, core), (swap, 1 - core)):
            chip = lax.rem(y + jnp.where(parity == 0, d, YS - d), YS)
            at_rows = pl.ds(pl.multiple_of((2 * chip + parity) * rows, rows), rows)
            out[d] = adam(total[at_rows, :], scale, m_ref[at_rows, :], v_ref[at_rows, :], r_ref[at_rows, :])

    if lead:

        @pl.when(i == pl.num_programs(0) - 1)
        def _():
            pltpu.make_async_copy(act_t, act_out, asem).wait()


def last_pseudo(lead, where, xp, gp, act, w, acc, m, v, hidden_scale):
    n = len(gp)
    units, width = w.shape
    features = width // 2
    tokens = sum(p.shape[0] for p in gp)
    steps = features // COLS
    base = 0 if lead else steps
    block = pl.BlockSpec((units, COLS), lambda i, s: (0, i + base))
    outs = pl.BlockSpec((YS, units // SETS, COLS), lambda i, s: (0, 0, i))
    out_shape = [jax.ShapeDtypeStruct((YS, units // SETS, features), BF16)] * 2
    tok = pltpu.VMEM((tokens, features), BF16)
    total = pltpu.VMEM((units, COLS), F32)
    hid = pltpu.VMEM((units, tokens), BF16)
    sems = pltpu.SemaphoreType.DMA((n,))
    one = pltpu.SemaphoreType.DMA
    if lead:
        head = (*xp, *gp, w)
        out_shape.append(jax.ShapeDtypeStruct((units, tokens), BF16))
        scratch = [total, tok, tok, pltpu.VMEM((units, width), BF16), hid, hid, sems, sems, one, one]
    else:
        head = (*gp, act)
        scratch = [total, tok, hid, sems, one]
    return pl.pallas_call(
        functools.partial(pseudo_kernel, n, lead, features, hidden_scale),
        grid_spec=pltpu.PrefetchScalarGridSpec(
            num_scalar_prefetch=1,
            grid=(steps,),
            in_specs=[ANY] * len(head) + [block] * 4,
            out_specs=[outs, outs] + ([ANY] if lead else []),
            scratch_shapes=scratch,
        ),
        out_shape=out_shape,
        compiler_params=pltpu.CompilerParams(vmem_limit_bytes=58 << 20),
        cost_estimate=pl.CostEstimate(
            flops=(6 if lead else 2) * tokens * units * features,
            bytes_accessed=units * features * 12 + tokens * width * 2,
            transcendentals=units * tokens,
        ),
        name="pseudo_in" if lead else "pseudo_out",
    )(where, *head, acc, m, v, w)


def assemble_kernel(halves, *refs):
    info = refs[0]
    out, sem = refs[-2:]
    ins = refs[1:-2]
    y, core = info[0], info[1]
    per = len(ins) // halves
    span = out.shape[2] // halves
    copies = []

    def copy(src, s, lo, n):
        dst = out.at[s, :, pl.ds(lo, n)]
        c = pltpu.make_async_copy(src, dst, sem.at[len(copies)])
        c.start()
        copies.append(c)

    def home(d, parity):
        return 2 * lax.rem(y + jnp.where(parity == 0, d, YS - d), YS) + parity

    for h in range(halves):
        own, nxt, far_l, far_r, prv, other = ins[h * per : (h + 1) * per]
        at = h * span
        copy(own.at[info[2]], home(0, core), at, span)
        copy(nxt.at[info[3]], home(1, core), at, span)
        copy(far_l.at[info[4]], home(2, core), at, span // 2)
        copy(far_r.at[info[4]], home(2, core), at + span // 2, span // 2)
        copy(prv.at[info[5]], home(3, core), at, span)
        for d in range(YS):
            copy(other.at[d], home(d, 1 - core), at, span)
    for c in copies:
        c.wait()


def assemble(info, pieces, rows, width):
    halves = len(pieces)
    flat = [a for p in pieces for a in p]
    return pl.pallas_call(
        functools.partial(assemble_kernel, halves),
        grid_spec=pltpu.PrefetchScalarGridSpec(
            num_scalar_prefetch=1,
            grid=(1,),
            in_specs=[pl.BlockSpec(memory_space=pltpu.VMEM)] * len(flat),
            out_specs=ANY,
            scratch_shapes=[pltpu.SemaphoreType.DMA((9 * halves,))],
        ),
        out_shape=jax.ShapeDtypeStruct((SETS, rows, width), BF16),
        name="assemble",
    )(info, *flat)


def per_device(
    input_activation_matrix,
    output_sensitivity,
    trajectory_initial_parameters,
    trajectory_gradient_average,
    trajectory_squared_average,
    common_expert_parameters,
    outer_inertia,
    trajectory_membership,
    punctual_flags,
):
    set_count, rows, width = trajectory_initial_parameters.shape[1:]
    units = set_count * rows
    features = width // 2
    hidden_scale = (SETS * UNIT) ** (-0.5)
    w = trajectory_initial_parameters[0].reshape(units, width)
    m = trajectory_gradient_average[0].reshape(units, width)
    v = trajectory_squared_average[0].reshape(units, width)

    me = lax.axis_index("path")
    y, core = me // 2, me % 2
    choices = common_expert_parameters.shape[1]
    eligible = jnp.arange(choices, dtype=jnp.int32)
    chosen = jnp.where(
        (trajectory_membership[:, :, None] == eligible[None, None, :])
        & (punctual_flags[:, None, None] == 1),
        1.0,
        0.0,
    ).astype(F32)
    steps = jnp.arange(YS, dtype=jnp.int32)
    ring_sets = 2 * ((y + jnp.where(core == 0, steps, YS - steps)) % YS) + core
    mine = chosen[me][ring_sets]
    mates = chosen[me ^ 1][ring_sets]
    tally = jnp.sum(chosen[:, me], axis=0)
    share = jnp.maximum(tally, 1.0)[:, None, None]
    own_pick = trajectory_membership[me][ring_sets]
    mate_pick = trajectory_membership[me ^ 1][ring_sets]
    where = jnp.stack([y, core]).astype(jnp.int32)

    calls = {
        0: ((-1, 0), (1, 0), (0, -1), (0, 1)),
        2: ((-1, -1), (1, 1), (-1, 1), (1, -1)),
        3: ((2, 0), (0, 2)),
        4: ((0, 0), (2, 2), (2, -1), (-1, 2)),
        5: ((2, 1), (1, 2)),
    }
    acc = None
    pending = None

    def compute(r, xb, gb):
        nonlocal acc, pending
        ready, pending = pending, None
        if r in calls and r < 5:
            acc = accumulate(
                [xb[b] for b in calls[r]], [gb[b] for b in calls[r]], w, acc, hidden_scale
            )
            pending = acc
        return ready

    xb, gb = gather_tokens(input_activation_matrix[0], output_sensitivity[0], compute)
    xl, gl = [xb[b] for b in calls[5]], [gb[b] for b in calls[5]]
    keep_in, swap_in, act = last_pseudo(True, where, xl, gl, None, w, acc, m, v, hidden_scale)
    keep_out, swap_out = last_pseudo(False, where, None, gl, act, w, acc, m, v, hidden_scale)

    common = common_expert_parameters[0]
    inertia = outer_inertia[0]
    mid = features // 2

    def refreshed(average, common, inertia):
        new_inertia = INERTIA_FACTOR * inertia + average
        return common - GLOBAL_LEARNING * (average + INERTIA_FACTOR * new_inertia), new_inertia

    totals, pieces = [], []
    mate = None
    for h, (keep, swap) in enumerate(((keep_in, swap_in), (keep_out, swap_out))):
        mate = on_path(swap if mate is None else after(swap, mate), 0, 1)

        def both(d, lo=0, hi=features, keep=keep, mate=mate):
            a = keep[d, :, lo:hi].astype(F32)[None]
            b = mate[d, :, lo:hi].astype(F32)[None]
            return mine[d][:, None, None] * a + mates[d][:, None, None] * b

        from_prv = on_path(both(2, 0, mid).astype(BF16), 1)
        from_nxt = on_path(both(2, mid, features).astype(BF16), -1)
        up = jnp.concatenate([both(1, 0, mid) + from_prv.astype(F32), both(1, mid, features)], -1)
        down = jnp.concatenate([both(3, 0, mid), both(3, mid, features) + from_nxt.astype(F32)], -1)
        part_up = on_path(up.astype(BF16), 1)
        part_down = on_path(down.astype(BF16), -1)
        total = both(0) + part_up.astype(F32) + part_down.astype(F32)
        totals.append(total)
        cols = slice(h * features, (h + 1) * features)
        experts, _ = refreshed(total / share, common[..., cols], inertia[..., cols])
        updated = experts.astype(BF16)
        prv, nxt = on_path(updated, 1), on_path(updated, -1)
        far_l = on_path(prv[..., :mid], 1)
        far_r = on_path(nxt[..., mid:], -1)
        far = jnp.concatenate([far_l, far_r], -1)
        chosen_for_mate = jnp.stack(
            [
                jnp.where(mate_pick[d] == 1, a[1], a[0])
                for d, a in enumerate((updated, nxt, far, prv))
            ]
        )
        other = on_path(chosen_for_mate, 0, 1)
        pieces.append((updated, nxt, far_l, far_r, prv, other))

    average = jnp.concatenate(totals, -1) / share
    new_experts, new_inertia = refreshed(average, common, inertia)
    info = jnp.concatenate([where, own_pick]).astype(jnp.int32)
    returned = assemble(info, pieces, rows, width)
    return (new_experts[None], new_inertia[None], returned[None])


def solution(mesh):
    placed = (
        P("path", "fsdp", None),
        P("path", "fsdp", None),
        P("path", None, "fsdp", None),
        P("path", None, "fsdp", None),
        P("path", None, "fsdp", None),
        P("path", None, "fsdp", None),
        P("path", None, "fsdp", None),
        P(),
        P(),
    )
    return jax.shard_map(
        per_device,
        mesh=mesh,
        in_specs=placed,
        out_specs=(
            P("path", None, "fsdp", None),
            P("path", None, "fsdp", None),
            P("path", None, "fsdp", None),
        ),
        check_vma=False,
    )
```

```python
import functools

import jax
import jax.numpy as jnp
from jax import lax
from jax.experimental import pallas as pl
from jax.experimental.pallas import tpu as pltpu
from jax.sharding import PartitionSpec as P

UNIT = 1024
SETS = 8
STEP = 1000


BETA_ONE = 0.9
BETA_TWO = 0.999
ADAM_EPS = 1e-08
INNER_RATE = 0.05
DECAY = 0.1
GLOBAL_LEARNING = 0.7
INERTIA_FACTOR = 0.9

ZS, XS, YS = 4, 4, 4
GELU_C = 0.7978845608028654
GELU_A = 0.044715
NT = (((1,), (1,)), ((), ()))
F32 = jnp.float32
BF16 = jnp.bfloat16
COLS = 512
CHUNK = 256
LIMIT = 46 << 20


def plane_hop(da, db):
    pairs = []
    for p in range(2 * YS):
        dz, dx = (da, db) if p % 2 == 0 else (db, da)
        for z in range(ZS):
            for x in range(XS):
                to = ((z + dz) % ZS) * XS + (x + dx) % XS
                pairs.append((p * ZS * XS + z * XS + x, p * ZS * XS + to))
    return pairs


def path_hop(hop, flip):
    return [
        (i, ((i // 2 + (hop if i % 2 == 0 else -hop)) % YS) * 2 + ((i % 2) ^ flip))
        for i in range(2 * YS)
    ]


def on_path(a, hop, flip=0):
    return lax.ppermute(a, "path", path_hop(hop, flip))


def after(a, *others):
    return lax.optimization_barrier((a, *others))[0]


def gather_tokens(x, g, compute):
    last = {}
    hold = []

    def send(a, da, db):
        nonlocal hold
        others = hold + ([last[da, db]] if (da, db) in last else [])
        if others:
            a = after(a, *others)
        out = lax.ppermute(a, ("path", "fsdp"), plane_hop(da, db))
        last[da, db] = out
        return out

    half = x.shape[0] // 2
    xb, gb = {(0, 0): x}, {(0, 0): g}
    xb[0, -1], xb[0, 1] = send(x, 0, 1), send(x, 0, -1)
    gb[-1, 0], gb[1, 0] = send(g, 1, 0), send(g, -1, 0)
    ups = [(-1, 0), (-1, -1), (-1, 1), (-1, 2), (2, 2), (2, 1)]
    downs = [(1, 0), (1, -1), (1, 1), (2, 0), (2, -1), (1, 2)]
    ends = [
        (xb[0, -1][:half], (0, 1)),
        (xb[0, 1][half:], (0, -1)),
        (gb[-1, 0][:half], (1, 0)),
        (gb[1, 0][half:], (-1, 0)),
    ]
    beside = {0: (0, 1), 1: (2,), 2: (3,)}
    parts = [None] * 4
    for r in range(6):
        if r in (1, 2):
            ends = [(after(p, xb[1, 0 if r == 1 else -1]), to) for p, to in ends]
        a, b = ups[r]
        c, d = downs[r]
        new = (
            send(xb[0 if a == -1 else -1, b], 1, 0),
            send(xb[0 if c == 1 else 1, d], -1, 0),
            send(gb[b, 0 if a == -1 else -1], 0, 1),
            send(gb[d, 0 if c == 1 else 1], 0, -1),
        )
        xb[a, b], xb[c, d], gb[b, a], gb[d, c] = new
        for k in beside.get(r, ()):
            parts[k] = lax.ppermute(ends[k][0], ("path", "fsdp"), plane_hop(*ends[k][1]))
        if r == 2:
            xb[0, 2] = jnp.concatenate(parts[:2], 0)
            gb[2, 0] = jnp.concatenate(parts[2:], 0)
        hold = [t for t in (compute(r, xb, gb),) if t is not None]
    return xb, gb


def hidden_both(xs, gs, w, act_t, dpre_t, features, hidden_scale):
    in_scale = features ** (-0.5)
    tokens = xs.shape[0]
    size = CHUNK if tokens % CHUNK == 0 else tokens

    def chunk(t, carry):
        rows = pl.ds(pl.multiple_of(t * size, size), size)
        pre = (
            lax.dot_general(w[:, :features], xs[rows, :], NT, preferred_element_type=F32)
            * in_scale
        )
        back = (
            lax.dot_general(w[:, features:], gs[rows, :], NT, preferred_element_type=F32)
            * hidden_scale
        )
        sq = pre * pre
        t_ = jnp.tanh(GELU_C * pre * (1.0 + GELU_A * sq))
        cdf = 0.5 * (1.0 + t_)
        slope = cdf + (0.5 * GELU_C) * pre * (1.0 - t_ * t_) * (1.0 + (3.0 * GELU_A) * sq)
        act_t[:, rows] = (pre * cdf).astype(BF16)
        dpre_t[:, rows] = (back * slope).astype(BF16)
        return carry

    lax.fori_loop(0, tokens // size, chunk, 0)


def stage(pieces, dst, sem):
    copies, at = [], 0
    for p in pieces:
        copies.append(pltpu.make_async_copy(p, dst.at[pl.ds(at, p.shape[0]), :], sem.at[len(copies)]))
        at += p.shape[0]
    return copies


def fetch(x_refs, g_refs, xs, gs, xsem, gsem):
    copies = stage(x_refs, xs, xsem) + stage(g_refs, gs, gsem)
    for c in copies:
        c.start()
    for c in copies:
        c.wait()


def grads_kernel(n, first, features, hidden_scale, *refs):
    x_refs, g_refs, w = refs[:n], refs[n : 2 * n], refs[2 * n]
    acc = None if first else refs[2 * n + 1]
    out, xs, gs, act_t, dpre_t, xsem, gsem = refs[-7:]
    fetch(x_refs, g_refs, xs, gs, xsem, gsem)
    hidden_both(xs, gs, w, act_t, dpre_t, features, hidden_scale)
    for left, right, base in ((dpre_t, xs, 0), (act_t, gs, features)):

        def columns(j, carry, left=left, right=right, base=base):
            term = jnp.dot(
                left[...],
                right[:, pl.ds(pl.multiple_of(j * COLS, COLS), COLS)],
                preferred_element_type=F32,
            )
            cols = pl.ds(pl.multiple_of(base + j * COLS, COLS), COLS)
            out[:, cols] = term if first else acc[:, cols] + term
            return carry

        lax.fori_loop(0, features // COLS, columns, 0)


ANY = pl.BlockSpec(memory_space=pl.ANY)
HBM = pl.BlockSpec(memory_space=pltpu.HBM)
VMEM = pl.BlockSpec(memory_space=pltpu.VMEM)


def accumulate(xp, gp, w, acc, hidden_scale):
    n = len(xp)
    units, width = w.shape
    features = width // 2
    tokens = sum(p.shape[0] for p in xp)
    first = acc is None
    return pl.pallas_call(
        functools.partial(grads_kernel, n, first, features, hidden_scale),
        in_specs=[HBM] * (2 * n) + [VMEM] * (1 if first else 2),
        out_specs=VMEM,
        out_shape=jax.ShapeDtypeStruct((units, width), F32),
        scratch_shapes=[
            pltpu.VMEM((tokens, features), BF16),
            pltpu.VMEM((tokens, features), BF16),
            pltpu.VMEM((units, tokens), BF16),
            pltpu.VMEM((units, tokens), BF16),
            pltpu.SemaphoreType.DMA((n,)),
            pltpu.SemaphoreType.DMA((n,)),
        ],
        input_output_aliases={} if first else {2 * n + 1: 0},
        compiler_params=pltpu.CompilerParams(vmem_limit_bytes=LIMIT),
        cost_estimate=pl.CostEstimate(
            flops=8 * tokens * units * features,
            bytes_accessed=tokens * width * 2,
            transcendentals=units * tokens,
        ),
        name="grads",
    )(*xp, *gp, w, *(() if first else (acc,)))


def adam(total, scale, first, second, start):
    corr_one = 1.0 - BETA_ONE**STEP
    corr_two = 1.0 - BETA_TWO**STEP
    raw = total * scale
    first_new = (INNER_RATE * BETA_ONE / corr_one) * first.astype(F32) + (
        INNER_RATE * (1.0 - BETA_ONE) / corr_one
    ) * raw
    second_new = (BETA_TWO / corr_two) * second.astype(F32) + (
        (1.0 - BETA_TWO) / corr_two
    ) * (raw * raw)
    root = second_new * lax.rsqrt(second_new)
    return (first_new / (root + ADAM_EPS) + (INNER_RATE * DECAY) * start.astype(F32)).astype(BF16)


def pseudo_kernel(n, lead, features, hidden_scale, *refs):
    where = refs[0]
    if lead:
        x_refs, g_refs = refs[1 : 1 + n], refs[1 + n : 1 + 2 * n]
        w, acc, m, v, keep, swap, act_t, total, dpre_t, xs, gs, xsem, gsem = refs[1 + 2 * n :]
        fetch(x_refs, g_refs, xs, gs, xsem, gsem)
        hidden_both(xs, gs, w, act_t, dpre_t, features, hidden_scale)
        left, right, base, scale = dpre_t, xs, 0, features ** (-0.5)
    else:
        g_refs, left = refs[1 : 1 + n], refs[1 + n]
        w, acc, m, v, keep, swap, total, right, gsem = refs[2 + n :]
        fetch((), g_refs, None, right, None, gsem)
        base, scale = features, hidden_scale
    y, core = where[0], where[1]
    rows = w.shape[0] // SETS

    def columns(j, carry):
        here = pl.ds(pl.multiple_of(j * COLS, COLS), COLS)
        cols = pl.ds(pl.multiple_of(base + j * COLS, COLS), COLS)
        total[...] = acc[:, cols] + jnp.dot(left[...], right[:, here], preferred_element_type=F32)

        def ring(d, carry):
            for out, parity in ((keep, core), (swap, 1 - core)):
                chip = lax.rem(y + jnp.where(parity == 0, d, YS - d), YS)
                at = pl.ds(pl.multiple_of((2 * chip + parity) * rows, rows), rows)
                out[d, :, here] = adam(total[at, :], scale, m[at, cols], v[at, cols], w[at, cols])
            return carry

        return lax.fori_loop(0, YS, ring, carry)

    lax.fori_loop(0, features // COLS, columns, 0)


def last_pseudo(lead, where, xp, gp, act, w, acc, m, v, hidden_scale):
    n = len(gp)
    units, width = w.shape
    features = width // 2
    tokens = sum(p.shape[0] for p in gp)
    out_shape = [jax.ShapeDtypeStruct((YS, units // SETS, features), BF16)] * 2
    tok = pltpu.VMEM((tokens, features), BF16)
    hid = pltpu.VMEM((units, tokens), BF16)
    sems = pltpu.SemaphoreType.DMA((n,))
    scratch = [pltpu.VMEM((units, COLS), F32)]
    if lead:
        head = (*xp, *gp)
        out_shape.append(jax.ShapeDtypeStruct((units, tokens), BF16))
        scratch += [hid, tok, tok, sems, sems]
    else:
        head = gp
        scratch += [tok, sems]
    tail = (() if lead else (act,)) + (w, acc, m, v)
    return pl.pallas_call(
        functools.partial(pseudo_kernel, n, lead, features, hidden_scale),
        in_specs=[pl.BlockSpec(memory_space=pltpu.SMEM)] + [HBM] * len(head) + [VMEM] * len(tail),
        out_specs=[VMEM] * len(out_shape),
        scratch_shapes=scratch,
        out_shape=out_shape,
        compiler_params=pltpu.CompilerParams(vmem_limit_bytes=LIMIT),
        cost_estimate=pl.CostEstimate(
            flops=(6 if lead else 2) * tokens * units * features,
            bytes_accessed=units * features * 12 + tokens * width * 2,
            transcendentals=units * tokens,
        ),
        name="pseudo_in" if lead else "pseudo_out",
    )(where, *head, *tail)


def assemble_kernel(halves, *refs):
    info = refs[0]
    out, sem = refs[-2:]
    ins = refs[1:-2]
    y, core = info[0], info[1]
    per = len(ins) // halves
    span = out.shape[2] // halves
    copies = []

    def copy(src, s, lo, n):
        dst = out.at[s, :, pl.ds(lo, n)]
        c = pltpu.make_async_copy(src, dst, sem.at[len(copies)])
        c.start()
        copies.append(c)

    def home(d, parity):
        return 2 * lax.rem(y + jnp.where(parity == 0, d, YS - d), YS) + parity

    for h in range(halves):
        own, nxt, far_l, far_r, prv, other = ins[h * per : (h + 1) * per]
        at = h * span
        copy(own.at[info[2]], home(0, core), at, span)
        copy(nxt.at[info[3]], home(1, core), at, span)
        copy(far_l.at[info[4]], home(2, core), at, span // 2)
        copy(far_r.at[info[4]], home(2, core), at + span // 2, span // 2)
        copy(prv.at[info[5]], home(3, core), at, span)
        for d in range(YS):
            copy(other.at[d], home(d, 1 - core), at, span)
    for c in copies:
        c.wait()


def assemble(info, pieces, rows, width):
    halves = len(pieces)
    flat = [a for p in pieces for a in p]
    return pl.pallas_call(
        functools.partial(assemble_kernel, halves),
        grid_spec=pltpu.PrefetchScalarGridSpec(
            num_scalar_prefetch=1,
            grid=(1,),
            in_specs=[pl.BlockSpec(memory_space=pltpu.VMEM)] * len(flat),
            out_specs=ANY,
            scratch_shapes=[pltpu.SemaphoreType.DMA((9 * halves,))],
        ),
        out_shape=jax.ShapeDtypeStruct((SETS, rows, width), BF16),
        name="assemble",
    )(info, *flat)


def per_device(
    input_activation_matrix,
    output_sensitivity,
    trajectory_initial_parameters,
    trajectory_gradient_average,
    trajectory_squared_average,
    common_expert_parameters,
    outer_inertia,
    trajectory_membership,
    punctual_flags,
):
    set_count, rows, width = trajectory_initial_parameters.shape[1:]
    units = set_count * rows
    features = width // 2
    hidden_scale = (SETS * UNIT) ** (-0.5)
    w = trajectory_initial_parameters[0].reshape(units, width)
    m = trajectory_gradient_average[0].reshape(units, width)
    v = trajectory_squared_average[0].reshape(units, width)

    me = lax.axis_index("path")
    y, core = me // 2, me % 2
    choices = common_expert_parameters.shape[1]
    eligible = jnp.arange(choices, dtype=jnp.int32)
    chosen = jnp.where(
        (trajectory_membership[:, :, None] == eligible[None, None, :])
        & (punctual_flags[:, None, None] == 1),
        1.0,
        0.0,
    ).astype(F32)
    steps = jnp.arange(YS, dtype=jnp.int32)
    ring_sets = 2 * ((y + jnp.where(core == 0, steps, YS - steps)) % YS) + core
    mine = chosen[me][ring_sets]
    mates = chosen[me ^ 1][ring_sets]
    tally = jnp.sum(chosen[:, me], axis=0)
    share = jnp.maximum(tally, 1.0)[:, None, None]
    own_pick = trajectory_membership[me][ring_sets]
    mate_pick = trajectory_membership[me ^ 1][ring_sets]
    where = jnp.stack([y, core]).astype(jnp.int32)

    calls = {
        0: ((-1, 0), (1, 0), (0, -1), (0, 1)),
        2: ((-1, -1), (1, 1), (-1, 1), (1, -1)),
        3: ((2, 0), (0, 2)),
        4: ((0, 0), (2, 2), (2, -1), (-1, 2)),
        5: ((2, 1), (1, 2)),
    }
    acc = None
    pending = None

    def compute(r, xb, gb):
        nonlocal acc, pending
        ready, pending = pending, None
        if r in calls and r < 5:
            acc = accumulate(
                [xb[b] for b in calls[r]], [gb[b] for b in calls[r]], w, acc, hidden_scale
            )
            pending = acc
        return ready

    xb, gb = gather_tokens(input_activation_matrix[0], output_sensitivity[0], compute)
    xl, gl = [xb[b] for b in calls[5]], [gb[b] for b in calls[5]]
    keep_in, swap_in, act = last_pseudo(True, where, xl, gl, None, w, acc, m, v, hidden_scale)
    keep_out, swap_out = last_pseudo(False, where, None, gl, act, w, acc, m, v, hidden_scale)

    common = common_expert_parameters[0]
    inertia = outer_inertia[0]
    mid = features // 2

    def refreshed(average, common, inertia):
        new_inertia = INERTIA_FACTOR * inertia + average
        return common - GLOBAL_LEARNING * (average + INERTIA_FACTOR * new_inertia), new_inertia

    totals, pieces = [], []
    mate = None
    for h, (keep, swap) in enumerate(((keep_in, swap_in), (keep_out, swap_out))):
        mate = on_path(swap if mate is None else after(swap, mate), 0, 1)

        def both(d, lo=0, hi=features, keep=keep, mate=mate):
            a = keep[d, :, lo:hi].astype(F32)[None]
            b = mate[d, :, lo:hi].astype(F32)[None]
            return mine[d][:, None, None] * a + mates[d][:, None, None] * b

        from_prv = on_path(both(2, 0, mid).astype(BF16), 1)
        from_nxt = on_path(both(2, mid, features).astype(BF16), -1)
        up = jnp.concatenate([both(1, 0, mid) + from_prv.astype(F32), both(1, mid, features)], -1)
        down = jnp.concatenate([both(3, 0, mid), both(3, mid, features) + from_nxt.astype(F32)], -1)
        part_up = on_path(up.astype(BF16), 1)
        part_down = on_path(down.astype(BF16), -1)
        total = both(0) + part_up.astype(F32) + part_down.astype(F32)
        totals.append(total)
        cols = slice(h * features, (h + 1) * features)
        experts, _ = refreshed(total / share, common[..., cols], inertia[..., cols])
        updated = experts.astype(BF16)
        prv, nxt = on_path(updated, 1), on_path(updated, -1)
        far_l = on_path(prv[..., :mid], 1)
        far_r = on_path(nxt[..., mid:], -1)
        far = jnp.concatenate([far_l, far_r], -1)
        chosen_for_mate = jnp.stack(
            [
                jnp.where(mate_pick[d] == 1, a[1], a[0])
                for d, a in enumerate((updated, nxt, far, prv))
            ]
        )
        other = on_path(chosen_for_mate, 0, 1)
        pieces.append((updated, nxt, far_l, far_r, prv, other))

    average = jnp.concatenate(totals, -1) / share
    new_experts, new_inertia = refreshed(average, common, inertia)
    info = jnp.concatenate([where, own_pick]).astype(jnp.int32)
    returned = assemble(info, pieces, rows, width)
    return (new_experts[None], new_inertia[None], returned[None])


def solution(mesh):
    placed = (
        P("path", "fsdp", None),
        P("path", "fsdp", None),
        P("path", None, "fsdp", None),
        P("path", None, "fsdp", None),
        P("path", None, "fsdp", None),
        P("path", None, "fsdp", None),
        P("path", None, "fsdp", None),
        P(),
        P(),
    )
    return jax.shard_map(
        per_device,
        mesh=mesh,
        in_specs=placed,
        out_specs=(
            P("path", None, "fsdp", None),
            P("path", None, "fsdp", None),
            P("path", None, "fsdp", None),
        ),
        check_vma=False,
    )
```

```python
import functools

import jax
import jax.numpy as jnp
from jax import lax
from jax.experimental import pallas as pl
from jax.experimental.pallas import tpu as pltpu
from jax.sharding import PartitionSpec as P

UNIT = 1024
SETS = 8
STEP = 1000


BETA_ONE = 0.9
BETA_TWO = 0.999
ADAM_EPS = 1e-08
INNER_RATE = 0.05
DECAY = 0.1
GLOBAL_LEARNING = 0.7
INERTIA_FACTOR = 0.9

ZS, XS, YS = 4, 4, 4
GELU_C = 0.7978845608028654
GELU_A = 0.044715
NT = (((1,), (1,)), ((), ()))
F32 = jnp.float32
BF16 = jnp.bfloat16
COLS = 512
CHUNK = 256
LIMIT = 46 << 20


def plane_hop(da, db):
    pairs = []
    for p in range(2 * YS):
        dz, dx = (da, db) if p % 2 == 0 else (db, da)
        for z in range(ZS):
            for x in range(XS):
                to = ((z + dz) % ZS) * XS + (x + dx) % XS
                pairs.append((p * ZS * XS + z * XS + x, p * ZS * XS + to))
    return pairs


def path_hop(hop, flip):
    return [
        (i, ((i // 2 + (hop if i % 2 == 0 else -hop)) % YS) * 2 + ((i % 2) ^ flip))
        for i in range(2 * YS)
    ]


def on_path(a, hop, flip=0):
    return lax.ppermute(a, "path", path_hop(hop, flip))


def after(a, *others):
    return lax.optimization_barrier((a, *others))[0]


def gather_tokens(own, compute):
    def send(a, to, *others):
        if others:
            a = after(a, *others)
        return lax.ppermute(a, ("path", "fsdp"), plane_hop(*to))

    half = own.shape[0] // 2
    got = {(0, 0): own}
    got[0, -1], got[0, 1] = send(own, (0, 1)), send(own, (0, -1))
    got[-1, 0], got[1, 0] = send(own, (1, 0)), send(own, (-1, 0))
    low = send(got[0, -1][:half], (0, 1))
    high = send(got[0, 1][half:], (0, -1))
    got[-1, -1] = send(got[0, -1], (1, 0), got[0, 1])
    got[1, -1] = send(got[0, -1], (-1, 0), got[0, 1])
    got[0, 2] = jnp.concatenate([low, high], 0)
    hold = {3: compute(0, got)}
    ups = [(-1, 0), (-1, -1), (-1, 1), (-1, 2), (2, 0), (2, -1)]
    downs = [(1, 0), (1, -1), (1, 1), (1, 2), (2, 1), (2, 2)]
    for j in range(2, 6):
        a, b = ups[j]
        c, d = downs[j]
        wait = [got[ups[j - 2]], got[downs[j - 2]]]
        if j == 2:
            wait += [low, high]
        if j == 4:
            hold[4] = compute(1, got)
        if j in hold:
            wait.append(hold[j])
        got[a, b] = send(got[0 if a == -1 else -1, b], (1, 0), *wait)
        got[c, d] = send(got[0 if c == 1 else 1, d], (-1, 0), *wait)
    compute(2, got)
    compute(3, got)
    return got


def hidden_both(xg, w, act_t, dpre_t, features, hidden_scale):
    in_scale = features ** (-0.5)
    tokens = xg.shape[0]
    size = CHUNK if tokens % CHUNK == 0 else tokens

    def chunk(t, carry):
        rows = pl.ds(pl.multiple_of(t * size, size), size)
        pre = (
            lax.dot_general(w[:, :features], xg[rows, :features], NT, preferred_element_type=F32)
            * in_scale
        )
        back = (
            lax.dot_general(w[:, features:], xg[rows, features:], NT, preferred_element_type=F32)
            * hidden_scale
        )
        sq = pre * pre
        t_ = jnp.tanh(GELU_C * pre * (1.0 + GELU_A * sq))
        cdf = 0.5 * (1.0 + t_)
        slope = cdf + (0.5 * GELU_C) * pre * (1.0 - t_ * t_) * (1.0 + (3.0 * GELU_A) * sq)
        act_t[:, rows] = (pre * cdf).astype(BF16)
        dpre_t[:, rows] = (back * slope).astype(BF16)
        return carry

    lax.fori_loop(0, tokens // size, chunk, 0)


def fetch(refs, dst, sem, cols=slice(None)):
    copies, at = [], 0
    for k, p in enumerate(refs):
        rows = pl.ds(at, p.shape[0])
        copies.append(pltpu.make_async_copy(p.at[:, cols], dst.at[rows, :], sem.at[k]))
        at += p.shape[0]
    for c in copies:
        c.start()
    for c in copies:
        c.wait()


def grads_kernel(n, first, features, hidden_scale, *refs):
    w, acc = refs[n], None if first else refs[n + 1]
    out, xg, act_t, dpre_t, sem = refs[-5:]
    fetch(refs[:n], xg, sem)
    hidden_both(xg, w, act_t, dpre_t, features, hidden_scale)
    for left, base in ((dpre_t, 0), (act_t, features)):

        def columns(j, carry, left=left, base=base):
            cols = pl.ds(pl.multiple_of(base + j * COLS, COLS), COLS)
            term = jnp.dot(left[...], xg[:, cols], preferred_element_type=F32)
            out[:, cols] = term if first else acc[:, cols] + term
            return carry

        lax.fori_loop(0, features // COLS, columns, 0)


ANY = pl.BlockSpec(memory_space=pl.ANY)
HBM = pl.BlockSpec(memory_space=pltpu.HBM)
VMEM = pl.BlockSpec(memory_space=pltpu.VMEM)


def resident(a):
    return pltpu.with_memory_space_constraint(a, pltpu.VMEM)


def accumulate(pieces, w, acc, hidden_scale):
    n = len(pieces)
    units, width = w.shape
    features = width // 2
    tokens = sum(p.shape[0] for p in pieces)
    first = acc is None
    return pl.pallas_call(
        functools.partial(grads_kernel, n, first, features, hidden_scale),
        in_specs=[HBM] * n + [VMEM] * (1 if first else 2),
        out_specs=VMEM,
        out_shape=pltpu.VMEM((units, width), F32),
        scratch_shapes=[
            pltpu.VMEM((tokens, width), BF16),
            pltpu.VMEM((units, tokens), BF16),
            pltpu.VMEM((units, tokens), BF16),
            pltpu.SemaphoreType.DMA((n,)),
        ],
        input_output_aliases={} if first else {n + 1: 0},
        compiler_params=pltpu.CompilerParams(vmem_limit_bytes=LIMIT),
        cost_estimate=pl.CostEstimate(
            flops=8 * tokens * units * features,
            bytes_accessed=tokens * width * 2,
            transcendentals=units * tokens,
        ),
        name="grads",
    )(*pieces, w, *(() if first else (acc,)))


def adam(total, scale, first, second, start):
    corr_one = 1.0 - BETA_ONE**STEP
    corr_two = 1.0 - BETA_TWO**STEP
    raw = total * scale
    first_new = (INNER_RATE * BETA_ONE / corr_one) * first.astype(F32) + (
        INNER_RATE * (1.0 - BETA_ONE) / corr_one
    ) * raw
    second_new = (BETA_TWO / corr_two) * second.astype(F32) + (
        (1.0 - BETA_TWO) / corr_two
    ) * (raw * raw)
    root = second_new * lax.rsqrt(second_new)
    return (first_new / (root + ADAM_EPS) + (INNER_RATE * DECAY) * start.astype(F32)).astype(BF16)


def pseudo_kernel(n, lead, features, hidden_scale, *refs):
    where, pieces = refs[0], refs[1 : 1 + n]
    if lead:
        w, acc, m, v, keep, swap, act_t, total, dpre_t, right, sem = refs[1 + n :]
        fetch(pieces, right, sem)
        hidden_both(right, w, act_t, dpre_t, features, hidden_scale)
        left, base, scale = dpre_t, 0, features ** (-0.5)
    else:
        left, w, acc, m, v, keep, swap, total, right, sem = refs[1 + n :]
        base, scale = features, hidden_scale
        fetch(pieces, right, sem, pl.ds(base, features))
    y, core = where[0], where[1]
    rows = w.shape[0] // SETS

    def columns(j, carry):
        here = pl.ds(pl.multiple_of(j * COLS, COLS), COLS)
        cols = pl.ds(pl.multiple_of(base + j * COLS, COLS), COLS)
        total[...] = acc[:, cols] + jnp.dot(left[...], right[:, here], preferred_element_type=F32)

        def ring(d, carry):
            for out, parity in ((keep, core), (swap, 1 - core)):
                chip = lax.rem(y + jnp.where(parity == 0, d, YS - d), YS)
                at = pl.ds(pl.multiple_of((2 * chip + parity) * rows, rows), rows)
                out[d, :, here] = adam(total[at, :], scale, m[at, cols], v[at, cols], w[at, cols])
            return carry

        return lax.fori_loop(0, YS, ring, carry)

    lax.fori_loop(0, features // COLS, columns, 0)


def last_pseudo(lead, where, pieces, act, w, acc, m, v, hidden_scale):
    n = len(pieces)
    units, width = w.shape
    features = width // 2
    tokens = sum(p.shape[0] for p in pieces)
    hid = (units, tokens)
    out_shape = [pltpu.VMEM((YS, units // SETS, features), BF16)] * 2
    scratch = [pltpu.VMEM((units, COLS), F32)]
    if lead:
        out_shape.append(pltpu.VMEM(hid, BF16))
        scratch += [pltpu.VMEM(hid, BF16), pltpu.VMEM((tokens, width), BF16)]
    else:
        scratch += [pltpu.VMEM((tokens, features), BF16)]
    tail = (() if lead else (act,)) + (w, acc, m, v)
    return pl.pallas_call(
        functools.partial(pseudo_kernel, n, lead, features, hidden_scale),
        in_specs=[pl.BlockSpec(memory_space=pltpu.SMEM)] + [HBM] * n + [VMEM] * len(tail),
        out_specs=[VMEM] * len(out_shape),
        scratch_shapes=scratch + [pltpu.SemaphoreType.DMA((n,))],
        out_shape=out_shape,
        compiler_params=pltpu.CompilerParams(vmem_limit_bytes=LIMIT),
        cost_estimate=pl.CostEstimate(
            flops=(6 if lead else 2) * tokens * units * features,
            bytes_accessed=units * features * 12 + tokens * width * 2,
            transcendentals=units * tokens,
        ),
        name="pseudo_in" if lead else "pseudo_out",
    )(where, *pieces, *tail)


def assemble_kernel(halves, *refs):
    info = refs[0]
    out, sem = refs[-2:]
    ins = refs[1:-2]
    y, core = info[0], info[1]
    per = len(ins) // halves
    span = out.shape[2] // halves
    copies = []

    def copy(src, s, lo, n):
        dst = out.at[s, :, pl.ds(lo, n)]
        c = pltpu.make_async_copy(src, dst, sem.at[len(copies)])
        c.start()
        copies.append(c)

    def home(d, parity):
        return 2 * lax.rem(y + jnp.where(parity == 0, d, YS - d), YS) + parity

    for h in range(halves):
        own, nxt, far_l, far_r, prv, other = ins[h * per : (h + 1) * per]
        at = h * span
        copy(own.at[info[2]], home(0, core), at, span)
        copy(nxt.at[info[3]], home(1, core), at, span)
        copy(far_l.at[info[4]], home(2, core), at, span // 2)
        copy(far_r.at[info[4]], home(2, core), at + span // 2, span // 2)
        copy(prv.at[info[5]], home(3, core), at, span)
        for d in range(YS):
            copy(other.at[d], home(d, 1 - core), at, span)
    for c in copies:
        c.wait()


def assemble(info, pieces, rows, width):
    halves = len(pieces)
    flat = [a for p in pieces for a in p]
    return pl.pallas_call(
        functools.partial(assemble_kernel, halves),
        grid_spec=pltpu.PrefetchScalarGridSpec(
            num_scalar_prefetch=1,
            grid=(1,),
            in_specs=[pl.BlockSpec(memory_space=pltpu.VMEM)] * len(flat),
            out_specs=ANY,
            scratch_shapes=[pltpu.SemaphoreType.DMA((9 * halves,))],
        ),
        out_shape=jax.ShapeDtypeStruct((SETS, rows, width), BF16),
        name="assemble",
    )(info, *flat)


def per_device(
    input_activation_matrix,
    output_sensitivity,
    trajectory_initial_parameters,
    trajectory_gradient_average,
    trajectory_squared_average,
    common_expert_parameters,
    outer_inertia,
    trajectory_membership,
    punctual_flags,
):
    set_count, rows, width = trajectory_initial_parameters.shape[1:]
    units = set_count * rows
    features = width // 2
    hidden_scale = (SETS * UNIT) ** (-0.5)
    w = trajectory_initial_parameters[0].reshape(units, width)
    m = trajectory_gradient_average[0].reshape(units, width)
    v = trajectory_squared_average[0].reshape(units, width)

    me = lax.axis_index("path")
    y, core = me // 2, me % 2
    choices = common_expert_parameters.shape[1]
    eligible = jnp.arange(choices, dtype=jnp.int32)
    chosen = jnp.where(
        (trajectory_membership[:, :, None] == eligible[None, None, :])
        & (punctual_flags[:, None, None] == 1),
        1.0,
        0.0,
    ).astype(F32)
    steps = jnp.arange(YS, dtype=jnp.int32)
    ring_sets = 2 * ((y + jnp.where(core == 0, steps, YS - steps)) % YS) + core
    mine = chosen[me][ring_sets]
    mates = chosen[me ^ 1][ring_sets]
    tally = jnp.sum(chosen[:, me], axis=0)
    share = jnp.maximum(tally, 1.0)[:, None, None]
    own_pick = trajectory_membership[me][ring_sets]
    mate_pick = trajectory_membership[me ^ 1][ring_sets]
    where = jnp.stack([y, core]).astype(jnp.int32)

    calls = (
        ((0, 0), (0, -1), (0, 1), (0, 2)),
        ((-1, 0), (1, 0), (-1, -1), (1, -1)),
        ((-1, 1), (1, 1), (-1, 2), (1, 2)),
        ((2, 0), (2, 1)),
    )
    small = (where, mine, mates, share, own_pick, mate_pick)
    w, where, mine, mates, share, own_pick, mate_pick = lax.optimization_barrier((w, *small))
    w, m, v = resident(w), resident(m), resident(v)
    acc = None

    def compute(k, got):
        nonlocal acc
        acc = accumulate([got[b] for b in calls[k]], w, acc, hidden_scale)
        return acc

    own = jnp.concatenate([input_activation_matrix[0], output_sensitivity[0]], 1)
    got = gather_tokens(own, compute)
    rest = [got[2, -1], got[2, 2]]
    keep_in, swap_in, act = last_pseudo(True, where, rest, None, w, acc, m, v, hidden_scale)
    keep_out, swap_out = last_pseudo(False, where, rest, act, w, acc, m, v, hidden_scale)

    common = common_expert_parameters[0]
    inertia = outer_inertia[0]
    mid = features // 2

    def refreshed(average, common, inertia):
        new_inertia = INERTIA_FACTOR * inertia + average
        return common - GLOBAL_LEARNING * (average + INERTIA_FACTOR * new_inertia), new_inertia

    totals, pieces = [], []
    mate = None
    for h, (keep, swap) in enumerate(((keep_in, swap_in), (keep_out, swap_out))):
        mate = on_path(swap if mate is None else after(swap, mate), 0, 1)

        def both(d, lo=0, hi=features, keep=keep, mate=mate):
            a = keep[d, :, lo:hi].astype(F32)[None]
            b = mate[d, :, lo:hi].astype(F32)[None]
            return mine[d][:, None, None] * a + mates[d][:, None, None] * b

        from_prv = on_path(both(2, 0, mid).astype(BF16), 1)
        from_nxt = on_path(both(2, mid, features).astype(BF16), -1)
        up = jnp.concatenate([both(1, 0, mid) + from_prv.astype(F32), both(1, mid, features)], -1)
        down = jnp.concatenate([both(3, 0, mid), both(3, mid, features) + from_nxt.astype(F32)], -1)
        part_up = on_path(up.astype(BF16), 1)
        part_down = on_path(down.astype(BF16), -1)
        total = both(0) + part_up.astype(F32) + part_down.astype(F32)
        totals.append(total)
        cols = slice(h * features, (h + 1) * features)
        experts, _ = refreshed(total / share, common[..., cols], inertia[..., cols])
        updated = experts.astype(BF16)
        prv, nxt = on_path(updated, 1), on_path(updated, -1)
        far_l = on_path(prv[..., :mid], 1)
        far_r = on_path(nxt[..., mid:], -1)
        far = jnp.concatenate([far_l, far_r], -1)
        chosen_for_mate = jnp.stack(
            [
                jnp.where(mate_pick[d] == 1, a[1], a[0])
                for d, a in enumerate((updated, nxt, far, prv))
            ]
        )
        other = on_path(chosen_for_mate, 0, 1)
        pieces.append((updated, nxt, far_l, far_r, prv, other))

    average = jnp.concatenate(totals, -1) / share
    new_experts, new_inertia = refreshed(average, common, inertia)
    info = jnp.concatenate([where, own_pick]).astype(jnp.int32)
    returned = assemble(info, pieces, rows, width)
    return (new_experts[None], new_inertia[None], returned[None])


def solution(mesh):
    placed = (
        P("path", "fsdp", None),
        P("path", "fsdp", None),
        P("path", None, "fsdp", None),
        P("path", None, "fsdp", None),
        P("path", None, "fsdp", None),
        P("path", None, "fsdp", None),
        P("path", None, "fsdp", None),
        P(),
        P(),
    )
    return jax.shard_map(
        per_device,
        mesh=mesh,
        in_specs=placed,
        out_specs=(
            P("path", None, "fsdp", None),
            P("path", None, "fsdp", None),
            P("path", None, "fsdp", None),
        ),
        check_vma=False,
    )
```

```python
import functools

import jax
import jax.numpy as jnp
from jax import lax
from jax.experimental import pallas as pl
from jax.experimental.pallas import tpu as pltpu
from jax.sharding import PartitionSpec as P

UNIT = 1024
SETS = 8
STEP = 1000


BETA_ONE = 0.9
BETA_TWO = 0.999
ADAM_EPS = 1e-08
INNER_RATE = 0.05
DECAY = 0.1
GLOBAL_LEARNING = 0.7
INERTIA_FACTOR = 0.9

ZS, XS, YS = 4, 4, 4
GELU_C = 0.7978845608028654
GELU_A = 0.044715
NT = (((1,), (1,)), ((), ()))
F32 = jnp.float32
BF16 = jnp.bfloat16
COLS = 512
CHUNK = 256
LIMIT = 30 << 20


def plane_hop(da, db):
    pairs = []
    for p in range(2 * YS):
        dz, dx = (da, db) if p % 2 == 0 else (db, da)
        for z in range(ZS):
            for x in range(XS):
                to = ((z + dz) % ZS) * XS + (x + dx) % XS
                pairs.append((p * ZS * XS + z * XS + x, p * ZS * XS + to))
    return pairs


def path_hop(hop, flip):
    return [
        (i, ((i // 2 + (hop if i % 2 == 0 else -hop)) % YS) * 2 + ((i % 2) ^ flip))
        for i in range(2 * YS)
    ]


def on_path(a, hop, flip=0):
    return lax.ppermute(a, "path", path_hop(hop, flip))


def after(a, *others):
    return lax.optimization_barrier((a, *others))[0]


def gather_tokens(x, g, compute):
    def send(a, to, *others):
        if others:
            a = after(a, *others)
        return lax.ppermute(a, ("path", "fsdp"), plane_hop(*to))

    def join(x, g):
        return jnp.concatenate([x, g], 1)

    x_prv, g_nxt = send(x, (0, 1)), send(g, (0, -1))
    x_nxt, g_prv = send(x, (0, -1)), send(g, (0, 1))
    x_far, g_far = send(x_prv, (0, 1)), send(g_nxt, (0, -1))
    own = join(x, g)
    got = {(0, 0): own, (0, -1): join(x_prv, g_prv), (0, 1): join(x_nxt, g_nxt)}
    got[0, 2] = join(x_far, g_far)
    got[-1, 0], got[1, 0] = send(own, (1, 0)), send(own, (-1, 0), x_prv)
    got[-1, -1] = send(got[0, -1], (1, 0), x_far, g_far)
    got[1, -1] = send(got[0, -1], (-1, 0), x_far, g_far)
    hold = {3: compute(0, got)}
    ups = [(-1, 0), (-1, -1), (-1, 1), (-1, 2), (2, 0), (2, -1)]
    downs = [(1, 0), (1, -1), (1, 1), (1, 2), (2, 1), (2, 2)]
    for j in range(2, 6):
        a, b = ups[j]
        c, d = downs[j]
        wait = [got[ups[j - 2]], got[downs[j - 2]]]
        if j == 4:
            hold[4] = compute(1, got)
        if j in hold:
            wait.append(hold[j])
        got[a, b] = send(got[0 if a == -1 else -1, b], (1, 0), *wait)
        got[c, d] = send(got[0 if c == 1 else 1, d], (-1, 0), *wait)
    compute(2, got)
    compute(3, got)
    return got


def hidden_both(xg, w, act_t, dpre_t, features, hidden_scale):
    in_scale = features ** (-0.5)
    tokens = xg.shape[0]
    size = CHUNK if tokens % CHUNK == 0 else tokens

    def chunk(t, carry):
        rows = pl.ds(pl.multiple_of(t * size, size), size)
        pre = (
            lax.dot_general(w[:, :features], xg[rows, :features], NT, preferred_element_type=F32)
            * in_scale
        )
        back = (
            lax.dot_general(w[:, features:], xg[rows, features:], NT, preferred_element_type=F32)
            * hidden_scale
        )
        sq = pre * pre
        t_ = jnp.tanh(GELU_C * pre * (1.0 + GELU_A * sq))
        cdf = 0.5 * (1.0 + t_)
        slope = cdf + (0.5 * GELU_C) * pre * (1.0 - t_ * t_) * (1.0 + (3.0 * GELU_A) * sq)
        act_t[:, rows] = (pre * cdf).astype(BF16)
        dpre_t[:, rows] = (back * slope).astype(BF16)
        return carry

    lax.fori_loop(0, tokens // size, chunk, 0)


def fetch(refs, dst, sem, cols=slice(None)):
    copies, at = [], 0
    for k, p in enumerate(refs):
        rows = pl.ds(at, p.shape[0])
        copies.append(pltpu.make_async_copy(p.at[:, cols], dst.at[rows, :], sem.at[k]))
        at += p.shape[0]
    for c in copies:
        c.start()
    for c in copies:
        c.wait()


def grads_kernel(n, first, features, hidden_scale, *refs):
    w, acc = refs[n], None if first else refs[n + 1]
    out, xg, act_t, dpre_t, sem = refs[-5:]
    fetch(refs[:n], xg, sem)
    hidden_both(xg, w, act_t, dpre_t, features, hidden_scale)
    for left, base in ((dpre_t, 0), (act_t, features)):

        def columns(j, carry, left=left, base=base):
            cols = pl.ds(pl.multiple_of(base + j * COLS, COLS), COLS)
            term = jnp.dot(left[...], xg[:, cols], preferred_element_type=F32)
            out[:, cols] = term if first else acc[:, cols] + term
            return carry

        lax.fori_loop(0, features // COLS, columns, 0)


ANY = pl.BlockSpec(memory_space=pl.ANY)
HBM = pl.BlockSpec(memory_space=pltpu.HBM)
VMEM = pl.BlockSpec(memory_space=pltpu.VMEM)


def resident(a):
    return pltpu.with_memory_space_constraint(a, pltpu.VMEM)


def accumulate(pieces, w, acc, hidden_scale):
    n = len(pieces)
    units, width = w.shape
    features = width // 2
    tokens = sum(p.shape[0] for p in pieces)
    first = acc is None
    return pl.pallas_call(
        functools.partial(grads_kernel, n, first, features, hidden_scale),
        in_specs=[HBM] * n + [VMEM] * (1 if first else 2),
        out_specs=VMEM,
        out_shape=pltpu.VMEM((units, width), F32),
        scratch_shapes=[
            pltpu.VMEM((tokens, width), BF16),
            pltpu.VMEM((units, tokens), BF16),
            pltpu.VMEM((units, tokens), BF16),
            pltpu.SemaphoreType.DMA((n,)),
        ],
        input_output_aliases={} if first else {n + 1: 0},
        compiler_params=pltpu.CompilerParams(vmem_limit_bytes=LIMIT),
        cost_estimate=pl.CostEstimate(
            flops=8 * tokens * units * features,
            bytes_accessed=tokens * width * 2,
            transcendentals=units * tokens,
        ),
        name="grads",
    )(*pieces, w, *(() if first else (acc,)))


def adam(total, scale, first, second, start):
    corr_one = 1.0 - BETA_ONE**STEP
    corr_two = 1.0 - BETA_TWO**STEP
    raw = total * scale
    first_new = (INNER_RATE * BETA_ONE / corr_one) * first.astype(F32) + (
        INNER_RATE * (1.0 - BETA_ONE) / corr_one
    ) * raw
    second_new = (BETA_TWO / corr_two) * second.astype(F32) + (
        (1.0 - BETA_TWO) / corr_two
    ) * (raw * raw)
    root = second_new * lax.rsqrt(second_new)
    return (first_new / (root + ADAM_EPS) + (INNER_RATE * DECAY) * start.astype(F32)).astype(BF16)


def pseudo_kernel(n, part, features, hidden_scale, *refs):
    where, pieces = refs[0], refs[1 : 1 + n]
    span = features if part == 0 else features // 2
    base, to = ((0, 0), (features, 0), (features + span, span))[part]
    if part == 0:
        w, acc, m, v, keep, swap, act_t, total, dpre_t, right, sem = refs[1 + n :]
        fetch(pieces, right, sem)
        hidden_both(right, w, act_t, dpre_t, features, hidden_scale)
        left, scale = dpre_t, features ** (-0.5)
    else:
        left, w, acc, m, v = refs[1 + n : 6 + n]
        keep, swap, total, right, sem = refs[-5:]
        scale = hidden_scale
        fetch(pieces, right, sem, pl.ds(base, span))
    y, core = where[0], where[1]
    rows = w.shape[0] // SETS

    def columns(j, carry):
        here = pl.ds(pl.multiple_of(j * COLS, COLS), COLS)
        put = pl.ds(pl.multiple_of(to + j * COLS, COLS), COLS)
        cols = pl.ds(pl.multiple_of(base + j * COLS, COLS), COLS)
        total[...] = acc[:, cols] + jnp.dot(left[...], right[:, here], preferred_element_type=F32)

        def ring(d, carry):
            for out, parity in ((keep, core), (swap, 1 - core)):
                chip = lax.rem(y + jnp.where(parity == 0, d, YS - d), YS)
                at = pl.ds(pl.multiple_of((2 * chip + parity) * rows, rows), rows)
                out[d, :, put] = adam(total[at, :], scale, m[at, cols], v[at, cols], w[at, cols])
            return carry

        return lax.fori_loop(0, YS, ring, carry)

    lax.fori_loop(0, span // COLS, columns, 0)


def last_pseudo(part, where, pieces, act, w, acc, m, v, begun, hidden_scale):
    n = len(pieces)
    units, width = w.shape
    features = width // 2
    span = features if part == 0 else features // 2
    tokens = sum(p.shape[0] for p in pieces)
    hid = (units, tokens)
    out_shape = [pltpu.VMEM((YS, units // SETS, features), BF16)] * 2
    scratch = [pltpu.VMEM((units, COLS), F32)]
    if part == 0:
        out_shape.append(pltpu.VMEM(hid, BF16))
        scratch += [pltpu.VMEM(hid, BF16), pltpu.VMEM((tokens, width), BF16)]
    else:
        scratch += [pltpu.VMEM((tokens, span), BF16)]
    tail = (() if part == 0 else (act,)) + (w, acc, m, v) + begun
    return pl.pallas_call(
        functools.partial(pseudo_kernel, n, part, features, hidden_scale),
        in_specs=[pl.BlockSpec(memory_space=pltpu.SMEM)] + [HBM] * n + [VMEM] * len(tail),
        out_specs=[VMEM] * len(out_shape),
        scratch_shapes=scratch + [pltpu.SemaphoreType.DMA((n,))],
        out_shape=out_shape,
        input_output_aliases={n + 6: 0, n + 7: 1} if begun else {},
        compiler_params=pltpu.CompilerParams(vmem_limit_bytes=LIMIT),
        cost_estimate=pl.CostEstimate(
            flops=(6 * features if part == 0 else 2 * span) * tokens * units,
            bytes_accessed=units * span * 12 + tokens * width * 2,
            transcendentals=units * tokens,
        ),
        name="pseudo_%d" % part,
    )(where, *pieces, *tail)


def home(info, d, parity):
    return 2 * lax.rem(info[0] + jnp.where(parity == 0, d, YS - d), YS) + parity


def own_kernel(halves, *refs):
    info, ins, out, sem = refs[0], refs[1:-2], refs[-2], refs[-1]
    per = len(ins) // halves
    span = out.shape[2] // halves
    copies = []

    def copy(src, d, lo, n):
        dst = out.at[home(info, d, info[1]), :, pl.ds(lo, n)]
        copies.append(pltpu.make_async_copy(src.at[info[2 + d]], dst, sem.at[len(copies)]))
        copies[-1].start()

    for h in range(halves):
        own, nxt, far_l, far_r, prv = ins[h * per : (h + 1) * per]
        at = h * span
        copy(own, 0, at, span)
        copy(nxt, 1, at, span)
        copy(far_l, 2, at, span // 2)
        copy(far_r, 2, at + span // 2, span // 2)
        copy(prv, 3, at, span)
    for c in copies:
        c.wait()


def other_kernel(halves, *refs):
    info, ins, out, sem = refs[0], refs[1 : 1 + halves], refs[-2], refs[-1]
    span = out.shape[2] // halves
    copies = []
    for h in range(halves):
        for d in range(YS):
            dst = out.at[home(info, d, 1 - info[1]), :, pl.ds(h * span, span)]
            copies.append(pltpu.make_async_copy(ins[h].at[d], dst, sem.at[h * YS + d]))
            copies[-1].start()
    for c in copies:
        c.wait()


def assemble(kernel, info, pieces, begun, halves, rows, width):
    return pl.pallas_call(
        functools.partial(kernel, halves),
        in_specs=[pl.BlockSpec(memory_space=pltpu.SMEM)]
        + [VMEM] * len(pieces)
        + [HBM] * len(begun),
        out_specs=HBM,
        out_shape=jax.ShapeDtypeStruct((SETS, rows, width), BF16),
        scratch_shapes=[pltpu.SemaphoreType.DMA((5 * halves,))],
        input_output_aliases={1 + len(pieces): 0} if begun else {},
        cost_estimate=pl.CostEstimate(
            flops=0, bytes_accessed=SETS * rows * width * 2, transcendentals=0
        ),
        name=kernel.__name__,
    )(info, *pieces, *begun)


def per_device(
    input_activation_matrix,
    output_sensitivity,
    trajectory_initial_parameters,
    trajectory_gradient_average,
    trajectory_squared_average,
    common_expert_parameters,
    outer_inertia,
    trajectory_membership,
    punctual_flags,
):
    set_count, rows, width = trajectory_initial_parameters.shape[1:]
    units = set_count * rows
    features = width // 2
    hidden_scale = (SETS * UNIT) ** (-0.5)
    w = trajectory_initial_parameters[0].reshape(units, width)
    m = trajectory_gradient_average[0].reshape(units, width)
    v = trajectory_squared_average[0].reshape(units, width)

    me = lax.axis_index("path")
    y, core = me // 2, me % 2
    choices = common_expert_parameters.shape[1]
    eligible = jnp.arange(choices, dtype=jnp.int32)
    chosen = jnp.where(
        (trajectory_membership[:, :, None] == eligible[None, None, :])
        & (punctual_flags[:, None, None] == 1),
        1.0,
        0.0,
    ).astype(F32)
    steps = jnp.arange(YS, dtype=jnp.int32)
    ring_sets = 2 * ((y + jnp.where(core == 0, steps, YS - steps)) % YS) + core
    mine = chosen[me][ring_sets]
    mates = chosen[me ^ 1][ring_sets]
    tally = jnp.sum(chosen[:, me], axis=0)
    share = jnp.maximum(tally, 1.0)[:, None, None]
    own_pick = trajectory_membership[me][ring_sets]
    mate_pick = trajectory_membership[me ^ 1][ring_sets]
    where = jnp.stack([y, core]).astype(jnp.int32)

    calls = (
        ((0, 0), (0, -1), (0, 1), (0, 2)),
        ((-1, 0), (1, 0), (-1, -1), (1, -1)),
        ((-1, 1), (1, 1), (-1, 2), (1, 2)),
        ((2, 0), (2, 1)),
    )
    small = (where, mine, mates, share, own_pick, mate_pick)
    w, where, mine, mates, share, own_pick, mate_pick = lax.optimization_barrier((w, *small))
    w, m, v = resident(w), resident(m), resident(v)
    acc = None

    def compute(k, got):
        nonlocal acc
        acc = accumulate([got[b] for b in calls[k]], w, acc, hidden_scale)
        return acc

    got = gather_tokens(input_activation_matrix[0], output_sensitivity[0], compute)
    rest = [got[2, -1], got[2, 2]]

    common = common_expert_parameters[0]
    inertia = outer_inertia[0]
    mid = features // 2

    def refreshed(average, common, inertia):
        new_inertia = INERTIA_FACTOR * inertia + average
        return common - GLOBAL_LEARNING * (average + INERTIA_FACTOR * new_inertia), new_inertia

    def merged(d, pair, lo=0, hi=features):
        keep, mate = (a[d, :, lo:hi].astype(F32)[None] for a in pair)
        return mine[d][:, None, None] * keep + mates[d][:, None, None] * mate

    def far_parts(pair):
        return merged(2, pair, 0, mid).astype(BF16), merged(2, pair, mid).astype(BF16)

    def far_sums(left, right):
        return on_path(left, 1), on_path(right, -1)

    def near_parts(pair, from_prv, from_nxt):
        up = [merged(1, pair, 0, mid) + from_prv.astype(F32), merged(1, pair, mid)]
        down = [merged(3, pair, 0, mid), merged(3, pair, mid) + from_nxt.astype(F32)]
        return [jnp.concatenate(p, -1).astype(BF16) for p in (up, down)]

    def near_sums(up, down):
        return on_path(up, 1), on_path(down, -1)

    def total_of(pair, parts):
        return merged(0, pair) + parts[0].astype(F32) + parts[1].astype(F32)

    def update(h, total):
        cols = slice(h * features, (h + 1) * features)
        return refreshed(total / share, common[..., cols], inertia[..., cols])[0].astype(BF16)

    def near_modules(updated):
        return on_path(updated, 1), on_path(updated, -1)

    def spread(updated, prv, nxt):
        far_l, far_r = on_path(prv[..., :mid], 1), on_path(nxt[..., mid:], -1)
        far = jnp.concatenate([far_l, far_r], -1)
        picked = [
            jnp.where(mate_pick[d] == 1, a[1], a[0]) for d, a in enumerate((updated, nxt, far, prv))
        ]
        return (updated, nxt, far_l, far_r, prv), on_path(jnp.stack(picked), 0, 1)

    acc = resident(acc)
    keep_0, swap_0, act = last_pseudo(0, where, rest, None, w, acc, m, v, (), hidden_scale)
    pair_0 = (keep_0, on_path(swap_0, 0, 1))
    act = resident(act)
    begun = last_pseudo(1, where, rest, act, w, acc, m, v, (), hidden_scale)
    pair_0 = (keep_0, after(pair_0[1], *begun))
    ends_0 = far_parts(pair_0)
    held = after(where, *ends_0)
    begun = tuple(resident(a) for a in begun)
    keep_1, swap_1 = last_pseudo(2, held, rest, act, w, acc, m, v, begun, hidden_scale)
    sums_0 = far_sums(*ends_0)
    pair_1 = (keep_1, on_path(after(swap_1, *sums_0), 0, 1))
    parts_0 = near_sums(*near_parts(pair_0, *sums_0))
    total_0 = total_of(pair_0, parts_0)
    sums_1 = far_sums(*far_parts(pair_1))
    updated_0 = update(0, total_0)
    near_0 = near_modules(updated_0)
    ends_1 = (after(a, *parts_0) for a in near_parts(pair_1, *sums_1))
    total_1 = total_of(pair_1, near_sums(*ends_1))
    updated_1 = update(1, after(total_1, *near_0))
    seen_0, other_0 = spread(updated_0, *near_0)
    seen_1, other_1 = spread(updated_1, *near_modules(updated_1))

    average = jnp.concatenate([total_0, total_1], -1) / share
    new_experts, new_inertia = refreshed(average, common, inertia)
    info = jnp.concatenate([where, own_pick]).astype(jnp.int32)
    returned = assemble(own_kernel, info, seen_0 + seen_1, (), 2, rows, width)
    returned = assemble(other_kernel, info, (other_0, other_1), (returned,), 2, rows, width)
    return (new_experts[None], new_inertia[None], returned[None])


def solution(mesh):
    placed = (
        P("path", "fsdp", None),
        P("path", "fsdp", None),
        P("path", None, "fsdp", None),
        P("path", None, "fsdp", None),
        P("path", None, "fsdp", None),
        P("path", None, "fsdp", None),
        P("path", None, "fsdp", None),
        P(),
        P(),
    )
    return jax.shard_map(
        per_device,
        mesh=mesh,
        in_specs=placed,
        out_specs=(
            P("path", None, "fsdp", None),
            P("path", None, "fsdp", None),
            P("path", None, "fsdp", None),
        ),
        check_vma=False,
    )
```

```python
import functools

import jax
import jax.numpy as jnp
from jax import lax
from jax.experimental import pallas as pl
from jax.experimental.pallas import tpu as pltpu
from jax.sharding import PartitionSpec as P

UNIT = 1024
SETS = 8
STEP = 1000


BETA_ONE = 0.9
BETA_TWO = 0.999
ADAM_EPS = 1e-08
INNER_RATE = 0.05
DECAY = 0.1
GLOBAL_LEARNING = 0.7
INERTIA_FACTOR = 0.9

ZS, XS, YS = 4, 4, 4
GELU_C = 0.7978845608028654
GELU_A = 0.044715
NT = (((1,), (1,)), ((), ()))
F32 = jnp.float32
BF16 = jnp.bfloat16
COLS = 512
CHUNK = 256
LIMIT = 30 << 20


def plane_hop(da, db):
    pairs = []
    for p in range(2 * YS):
        dz, dx = (da, db) if p % 2 == 0 else (db, da)
        for z in range(ZS):
            for x in range(XS):
                to = ((z + dz) % ZS) * XS + (x + dx) % XS
                pairs.append((p * ZS * XS + z * XS + x, p * ZS * XS + to))
    return pairs


def path_hop(hop, flip):
    return [
        (i, ((i // 2 + (hop if i % 2 == 0 else -hop)) % YS) * 2 + ((i % 2) ^ flip))
        for i in range(2 * YS)
    ]


def on_path(a, hop, flip=0):
    return lax.ppermute(a, "path", path_hop(hop, flip))


def after(a, *others):
    return lax.optimization_barrier((a, *others))[0]


def gather_tokens(x, g, compute):
    def send(a, to, *others):
        if others:
            a = after(a, *others)
        return lax.ppermute(a, ("path", "fsdp"), plane_hop(*to))

    def join(x, g):
        return jnp.concatenate([x, g], 1)

    x_prv, g_nxt = send(x, (0, 1)), send(g, (0, -1))
    x_nxt, g_prv = send(x, (0, -1)), send(g, (0, 1))
    x_far, g_far = send(x_prv, (0, 1)), send(g_nxt, (0, -1))
    own = join(x, g)
    got = {(0, 0): own, (0, -1): join(x_prv, g_prv), (0, 1): join(x_nxt, g_nxt)}
    got[0, 2] = join(x_far, g_far)
    got[-1, 0] = send(own, (1, 0), x_prv, g_nxt)
    got[1, 0] = send(own, (-1, 0), x_prv, g_nxt)
    got[-1, -1] = send(got[0, -1], (1, 0), x_far, g_far)
    got[1, -1] = send(got[0, -1], (-1, 0), x_far, g_far)
    hold = {3: compute(0, got)}
    ups = [(-1, 0), (-1, -1), (-1, 1), (-1, 2), (2, 0), (2, -1)]
    downs = [(1, 0), (1, -1), (1, 1), (1, 2), (2, 1), (2, 2)]
    for j in range(2, 6):
        a, b = ups[j]
        c, d = downs[j]
        wait = [got[ups[j - 2]], got[downs[j - 2]]]
        if j == 4:
            hold[4] = compute(1, got)
        if j in hold:
            wait.append(hold[j])
        got[a, b] = send(got[0 if a == -1 else -1, b], (1, 0), *wait)
        got[c, d] = send(got[0 if c == 1 else 1, d], (-1, 0), *wait)
    compute(2, got)
    compute(3, got)
    return got


def hidden_both(xg, w, act_t, dpre_t, features, hidden_scale):
    in_scale = features ** (-0.5)
    tokens = xg.shape[0]
    size = CHUNK if tokens % CHUNK == 0 else tokens

    def chunk(t, carry):
        rows = pl.ds(pl.multiple_of(t * size, size), size)
        pre = (
            lax.dot_general(w[:, :features], xg[rows, :features], NT, preferred_element_type=F32)
            * in_scale
        )
        back = (
            lax.dot_general(w[:, features:], xg[rows, features:], NT, preferred_element_type=F32)
            * hidden_scale
        )
        sq = pre * pre
        t_ = jnp.tanh(GELU_C * pre * (1.0 + GELU_A * sq))
        cdf = 0.5 * (1.0 + t_)
        slope = cdf + (0.5 * GELU_C) * pre * (1.0 - t_ * t_) * (1.0 + (3.0 * GELU_A) * sq)
        act_t[:, rows] = (pre * cdf).astype(BF16)
        dpre_t[:, rows] = (back * slope).astype(BF16)
        return carry

    lax.fori_loop(0, tokens // size, chunk, 0)


def fetch(refs, dst, sem, cols=slice(None)):
    copies, at = [], 0
    for k, p in enumerate(refs):
        rows = pl.ds(at, p.shape[0])
        copies.append(pltpu.make_async_copy(p.at[:, cols], dst.at[rows, :], sem.at[k]))
        at += p.shape[0]
    for c in copies:
        c.start()
    for c in copies:
        c.wait()


def grads_kernel(n, first, features, hidden_scale, *refs):
    w, acc = refs[n], None if first else refs[n + 1]
    out, xg, act_t, dpre_t, sem = refs[-5:]
    fetch(refs[:n], xg, sem)
    hidden_both(xg, w, act_t, dpre_t, features, hidden_scale)
    for left, base in ((dpre_t, 0), (act_t, features)):

        def columns(j, carry, left=left, base=base):
            cols = pl.ds(pl.multiple_of(base + j * COLS, COLS), COLS)
            term = jnp.dot(left[...], xg[:, cols], preferred_element_type=F32)
            out[:, cols] = term if first else acc[:, cols] + term
            return carry

        lax.fori_loop(0, features // COLS, columns, 0)


ANY = pl.BlockSpec(memory_space=pl.ANY)
HBM = pl.BlockSpec(memory_space=pltpu.HBM)
VMEM = pl.BlockSpec(memory_space=pltpu.VMEM)


def resident(a):
    return pltpu.with_memory_space_constraint(a, pltpu.VMEM)


def accumulate(pieces, w, acc, hidden_scale):
    n = len(pieces)
    units, width = w.shape
    features = width // 2
    tokens = sum(p.shape[0] for p in pieces)
    first = acc is None
    return pl.pallas_call(
        functools.partial(grads_kernel, n, first, features, hidden_scale),
        in_specs=[HBM] * n + [VMEM] * (1 if first else 2),
        out_specs=VMEM,
        out_shape=pltpu.VMEM((units, width), F32),
        scratch_shapes=[
            pltpu.VMEM((tokens, width), BF16),
            pltpu.VMEM((units, tokens), BF16),
            pltpu.VMEM((units, tokens), BF16),
            pltpu.SemaphoreType.DMA((n,)),
        ],
        input_output_aliases={} if first else {n + 1: 0},
        compiler_params=pltpu.CompilerParams(vmem_limit_bytes=LIMIT),
        cost_estimate=pl.CostEstimate(
            flops=8 * tokens * units * features,
            bytes_accessed=tokens * width * 2,
            transcendentals=units * tokens,
        ),
        name="grads",
    )(*pieces, w, *(() if first else (acc,)))


def adam(total, scale, first, second, start):
    corr_one = 1.0 - BETA_ONE**STEP
    corr_two = 1.0 - BETA_TWO**STEP
    raw = total * scale
    first_new = (INNER_RATE * BETA_ONE / corr_one) * first.astype(F32) + (
        INNER_RATE * (1.0 - BETA_ONE) / corr_one
    ) * raw
    second_new = (BETA_TWO / corr_two) * second.astype(F32) + (
        (1.0 - BETA_TWO) / corr_two
    ) * (raw * raw)
    root = second_new * lax.rsqrt(second_new)
    return (first_new / (root + ADAM_EPS) + (INNER_RATE * DECAY) * start.astype(F32)).astype(BF16)


def pseudo_kernel(n, part, features, hidden_scale, *refs):
    where, pieces = refs[0], refs[1 : 1 + n]
    base = part * features
    if part == 0:
        w, acc, m, v, keep, swap, far_keep, far_swap, act_t = refs[1 + n : 10 + n]
        total, dpre_t, right, sem = refs[10 + n :]
        fetch(pieces, right, sem)
        hidden_both(right, w, act_t, dpre_t, features, hidden_scale)
        left, scale = dpre_t, features ** (-0.5)
    else:
        left, w, acc, m, v, keep, swap, far_keep, far_swap, total, right, sem = refs[1 + n :]
        scale = hidden_scale
        fetch(pieces, right, sem, pl.ds(base, features))
    y, core = where[0], where[1]
    rows = w.shape[0] // SETS
    per = far_keep.shape[2] // COLS

    def columns(j, carry):
        here = pl.ds(pl.multiple_of(j * COLS, COLS), COLS)
        cols = pl.ds(pl.multiple_of(base + j * COLS, COLS), COLS)
        total[...] = acc[:, cols] + jnp.dot(left[...], right[:, here], preferred_element_type=F32)

        def stepped(d, parity):
            chip = lax.rem(y + jnp.where(parity == 0, d, YS - d), YS)
            at = pl.ds(pl.multiple_of((2 * chip + parity) * rows, rows), rows)
            return adam(total[at, :], scale, m[at, cols], v[at, cols], w[at, cols])

        def ring(i, carry):
            for out, parity in ((keep, core), (swap, 1 - core)):
                out[i, :, here] = stepped(i + i // 2, parity)
            return carry

        lax.fori_loop(0, YS - 1, ring, carry)
        put = pl.ds(pl.multiple_of(lax.rem(j, per) * COLS, COLS), COLS)
        for out, parity in ((far_keep, core), (far_swap, 1 - core)):
            out[lax.div(j, per), :, put] = stepped(2, parity)
        return carry

    lax.fori_loop(0, features // COLS, columns, 0)


def last_pseudo(part, where, pieces, act, w, acc, m, v, hidden_scale):
    n = len(pieces)
    units, width = w.shape
    features = width // 2
    rows = units // SETS
    tokens = sum(p.shape[0] for p in pieces)
    hid = (units, tokens)
    near = pltpu.VMEM((YS - 1, rows, features), BF16)
    far = pltpu.VMEM((2, rows, features // 2), BF16)
    out_shape = [near, near, far, far]
    scratch = [pltpu.VMEM((units, COLS), F32)]
    if part == 0:
        out_shape.append(pltpu.VMEM(hid, BF16))
        scratch += [pltpu.VMEM(hid, BF16), pltpu.VMEM((tokens, width), BF16)]
    else:
        scratch += [pltpu.VMEM((tokens, features), BF16)]
    tail = (() if part == 0 else (act,)) + (w, acc, m, v)
    return pl.pallas_call(
        functools.partial(pseudo_kernel, n, part, features, hidden_scale),
        in_specs=[pl.BlockSpec(memory_space=pltpu.SMEM)] + [HBM] * n + [VMEM] * len(tail),
        out_specs=[VMEM] * len(out_shape),
        scratch_shapes=scratch + [pltpu.SemaphoreType.DMA((n,))],
        out_shape=out_shape,
        compiler_params=pltpu.CompilerParams(vmem_limit_bytes=LIMIT),
        cost_estimate=pl.CostEstimate(
            flops=(6 if part == 0 else 2) * features * tokens * units,
            bytes_accessed=units * features * 12 + tokens * width * 2,
            transcendentals=units * tokens,
        ),
        name="pseudo_%d" % part,
    )(where, *pieces, *tail)


def home(info, d, parity):
    return 2 * lax.rem(info[0] + jnp.where(parity == 0, d, YS - d), YS) + parity


def run_copies(pairs, sem):
    copies = [pltpu.make_async_copy(a, b, sem.at[k]) for k, (a, b) in enumerate(pairs)]
    for c in copies:
        c.start()
    for c in copies:
        c.wait()


def near_own_kernel(info, own, nxt, prv, out, sem):
    run_copies(
        [(a.at[info[2 + d]], out.at[home(info, d, info[1])]) for a, d in ((own, 0), (nxt, 1), (prv, 3))],
        sem,
    )


def rest_kernel(info, near, own_l, own_r, other_l, other_r, begun, out, sem):
    half = own_l.shape[1]
    left, right = pl.ds(0, half), pl.ds(half, half)
    pairs = [(near.at[i], out.at[home(info, d, 1 - info[1])]) for i, d in enumerate((0, 1, 3))]
    for parity, l, r in ((info[1], own_l, own_r), (1 - info[1], other_l, other_r)):
        far = home(info, 2, parity)
        pairs += [(l, out.at[far, :, left]), (r, out.at[far, :, right])]
    run_copies(pairs, sem)


def assemble(kernel, info, pieces, begun, copies, rows, width):
    return pl.pallas_call(
        kernel,
        in_specs=[pl.BlockSpec(memory_space=pltpu.SMEM)]
        + [VMEM] * len(pieces)
        + [HBM] * len(begun),
        out_specs=HBM,
        out_shape=jax.ShapeDtypeStruct((SETS, rows, width), BF16),
        scratch_shapes=[pltpu.SemaphoreType.DMA((copies,))],
        input_output_aliases={1 + len(pieces): 0} if begun else {},
        cost_estimate=pl.CostEstimate(
            flops=0, bytes_accessed=SETS * rows * width * 2, transcendentals=0
        ),
        name=kernel.__name__,
    )(info, *pieces, *begun)


def per_device(
    input_activation_matrix,
    output_sensitivity,
    trajectory_initial_parameters,
    trajectory_gradient_average,
    trajectory_squared_average,
    common_expert_parameters,
    outer_inertia,
    trajectory_membership,
    punctual_flags,
):
    set_count, rows, width = trajectory_initial_parameters.shape[1:]
    units = set_count * rows
    features = width // 2
    hidden_scale = (SETS * UNIT) ** (-0.5)
    w = trajectory_initial_parameters[0].reshape(units, width)
    m = trajectory_gradient_average[0].reshape(units, width)
    v = trajectory_squared_average[0].reshape(units, width)

    me = lax.axis_index("path")
    y, core = me // 2, me % 2
    choices = common_expert_parameters.shape[1]
    eligible = jnp.arange(choices, dtype=jnp.int32)
    chosen = jnp.where(
        (trajectory_membership[:, :, None] == eligible[None, None, :])
        & (punctual_flags[:, None, None] == 1),
        1.0,
        0.0,
    ).astype(F32)
    turn = 1 - 2 * core
    chips = (y + turn * jnp.arange(YS, dtype=jnp.int32)) % YS
    sets = 2 * chips + core
    nxt_chip, prv_chip = chips[1], chips[3]
    mate = me ^ 1
    paths = jnp.stack(
        [me] * 4
        + [mate] * 4
        + [2 * prv_chip + core, 2 * prv_chip + 1 - core]
        + [2 * nxt_chip + core, 2 * nxt_chip + 1 - core]
    )
    at_sets = jnp.concatenate([sets, sets, sets[1:2], sets[1:2], sets[3:], sets[3:]])
    weights = chosen[paths, at_sets]
    pick_paths = jnp.concatenate([paths[:8], paths[10:], paths[8:10]])
    pick_sets = jnp.concatenate([sets, sets, sets[3:], sets[3:], sets[1:2], sets[1:2]])
    picks = trajectory_membership[pick_paths, pick_sets]
    tally = jnp.sum(chosen[:, me], axis=0)
    share = jnp.maximum(tally, 1.0)[:, None, None]
    where = jnp.stack([y, core]).astype(jnp.int32)
    info = jnp.concatenate([where, picks[:4]]).astype(jnp.int32)

    calls = (
        ((0, 0), (0, -1), (0, 1), (0, 2)),
        ((-1, 0), (1, 0), (-1, -1), (1, -1)),
        ((-1, 1), (1, 1), (-1, 2), (1, 2)),
        ((2, 0), (2, 1)),
    )
    w, where, weights, picks, share, info = lax.optimization_barrier(
        (w, where, weights, picks, share, info)
    )
    w, m, v = resident(w), resident(m), resident(v)
    acc = None

    def compute(k, got):
        nonlocal acc
        acc = accumulate([got[b] for b in calls[k]], w, acc, hidden_scale)
        return acc

    got = gather_tokens(input_activation_matrix[0], output_sensitivity[0], compute)
    rest = [got[2, -1], got[2, 2]]

    common = common_expert_parameters[0]
    inertia = outer_inertia[0]
    mid = features // 2

    def weighed(k, a):
        return weights[k][:, None, None] * a.astype(F32)[None]

    def exchange(swap, far_keep, far_swap):
        lefts = on_path(far_keep[0], 1), on_path(far_swap[0], -1, 1)
        rights = on_path(far_keep[1], -1), on_path(far_swap[1], 1, 1)
        return (on_path(swap, 0, 1), *lefts, *rights)

    def sums(keep, came):
        near = came[0]

        def merged(i, d, lo=0, hi=features):
            return weighed(d, keep[i, :, lo:hi]) + weighed(4 + d, near[i, :, lo:hi])

        up = [merged(1, 1, 0, mid) + weighed(8, came[1]) + weighed(9, came[2]), merged(1, 1, mid)]
        down = [merged(2, 3, 0, mid), merged(2, 3, mid) + weighed(10, came[3]) + weighed(11, came[4])]
        return merged(0, 0), up, down

    acc = resident(acc)
    keep_0, *out_0, act = last_pseudo(0, where, rest, None, w, acc, m, v, hidden_scale)
    came_0 = exchange(*out_0)
    keep_1, *out_1 = last_pseudo(1, where, rest, resident(act), w, acc, m, v, hidden_scale)
    came_1 = exchange(*lax.optimization_barrier((*out_1, *came_0))[:3])
    here_0, up_0, down_0 = sums(keep_0, came_0)
    here_1, up_1, down_1 = sums(keep_1, came_1)
    part_up = on_path(jnp.concatenate([a.astype(BF16) for a in up_0 + up_1], -1), 1)
    part_down = on_path(jnp.concatenate([a.astype(BF16) for a in down_0 + down_1], -1), -1)

    total = jnp.concatenate([here_0, here_1], -1) + part_up.astype(F32) + part_down.astype(F32)
    average = total / share
    new_inertia = INERTIA_FACTOR * inertia + average
    new_experts = common - GLOBAL_LEARNING * (average + INERTIA_FACTOR * new_inertia)
    updated = new_experts.astype(BF16)
    prv, nxt = on_path(updated, 1), on_path(updated, -1)

    def picked(k, a, lo=0, hi=width):
        return jnp.where(picks[k] == 1, a[1, :, lo:hi], a[0, :, lo:hi])

    own_l = on_path(picked(8, prv, 0, features), 1)
    other_l = on_path(picked(9, prv, 0, features), 1, 1)
    own_r = on_path(picked(10, nxt, features), -1)
    other_r = on_path(picked(11, nxt, features), -1, 1)
    near = on_path(jnp.stack([picked(4, updated), picked(5, nxt), picked(7, prv)]), 0, 1)
    returned = assemble(near_own_kernel, info, (updated, nxt, prv), (), 3, rows, width)
    far = (own_l, own_r, other_l, other_r)
    returned = assemble(rest_kernel, info, (near, *far), (returned,), 7, rows, width)
    return (new_experts[None], new_inertia[None], returned[None])


def solution(mesh):
    placed = (
        P("path", "fsdp", None),
        P("path", "fsdp", None),
        P("path", None, "fsdp", None),
        P("path", None, "fsdp", None),
        P("path", None, "fsdp", None),
        P("path", None, "fsdp", None),
        P("path", None, "fsdp", None),
        P(),
        P(),
    )
    return jax.shard_map(
        per_device,
        mesh=mesh,
        in_specs=placed,
        out_specs=(
            P("path", None, "fsdp", None),
            P("path", None, "fsdp", None),
            P("path", None, "fsdp", None),
        ),
        check_vma=False,
    )
```

```python
import functools

import jax
import jax.numpy as jnp
from jax import lax
from jax.experimental import pallas as pl
from jax.experimental.pallas import tpu as pltpu
from jax.sharding import PartitionSpec as P

UNIT = 1024
SETS = 8
STEP = 1000


BETA_ONE = 0.9
BETA_TWO = 0.999
ADAM_EPS = 1e-08
INNER_RATE = 0.05
DECAY = 0.1
GLOBAL_LEARNING = 0.7
INERTIA_FACTOR = 0.9

ZS, XS, YS = 4, 4, 4
GELU_C = 0.7978845608028654
GELU_A = 0.044715
NT = (((1,), (1,)), ((), ()))
F32 = jnp.float32
BF16 = jnp.bfloat16
COLS = 512
CHUNK = 256
LIMIT = 30 << 20


def plane_hop(da, db):
    pairs = []
    for p in range(2 * YS):
        dz, dx = (da, db) if p % 2 == 0 else (db, da)
        for z in range(ZS):
            for x in range(XS):
                to = ((z + dz) % ZS) * XS + (x + dx) % XS
                pairs.append((p * ZS * XS + z * XS + x, p * ZS * XS + to))
    return pairs


def path_hop(hop, flip):
    return [
        (i, ((i // 2 + (hop if i % 2 == 0 else -hop)) % YS) * 2 + ((i % 2) ^ flip))
        for i in range(2 * YS)
    ]


def on_path(a, hop, flip=0):
    return lax.ppermute(a, "path", path_hop(hop, flip))


def after(a, *others):
    return lax.optimization_barrier((a, *others))[0]


def gather_tokens(x, g, compute):
    def send(a, to, *others):
        if others:
            a = after(a, *others)
        return lax.ppermute(a, ("path", "fsdp"), plane_hop(*to))

    def join(x, g):
        return jnp.concatenate([x, g], 1)

    x_prv, g_nxt = send(x, (0, 1)), send(g, (0, -1))
    x_nxt, g_prv = send(x, (0, -1)), send(g, (0, 1))
    x_far, g_far = send(x_prv, (0, 1)), send(g_nxt, (0, -1))
    own = join(x, g)
    got = {(0, 0): own, (0, -1): join(x_prv, g_prv), (0, 1): join(x_nxt, g_nxt)}
    got[0, 2] = join(x_far, g_far)
    got[-1, 0] = send(own, (1, 0), x_prv, g_nxt)
    got[1, 0] = send(own, (-1, 0), x_prv, g_nxt)
    got[-1, -1] = send(got[0, -1], (1, 0), x_far, g_far)
    got[1, -1] = send(got[0, -1], (-1, 0), x_far, g_far)
    hold = {3: compute(0, got)}
    ups = [(-1, 0), (-1, -1), (-1, 1), (-1, 2), (2, 0), (2, -1)]
    downs = [(1, 0), (1, -1), (1, 1), (1, 2), (2, 1), (2, 2)]
    for j in range(2, 6):
        a, b = ups[j]
        c, d = downs[j]
        wait = [got[ups[j - 2]], got[downs[j - 2]]]
        if j == 4:
            hold[4] = compute(1, got)
        if j in hold:
            wait.append(hold[j])
        got[a, b] = send(got[0 if a == -1 else -1, b], (1, 0), *wait)
        got[c, d] = send(got[0 if c == 1 else 1, d], (-1, 0), *wait)
    compute(2, got)
    compute(3, got)
    return got


def hidden_both(xg, w, act_t, dpre_t, features, hidden_scale):
    in_scale = features ** (-0.5)
    tokens = xg.shape[0]
    size = CHUNK if tokens % CHUNK == 0 else tokens

    def chunk(t, carry):
        rows = pl.ds(pl.multiple_of(t * size, size), size)
        pre = (
            lax.dot_general(w[:, :features], xg[rows, :features], NT, preferred_element_type=F32)
            * in_scale
        )
        back = (
            lax.dot_general(w[:, features:], xg[rows, features:], NT, preferred_element_type=F32)
            * hidden_scale
        )
        sq = pre * pre
        t_ = jnp.tanh(GELU_C * pre * (1.0 + GELU_A * sq))
        cdf = 0.5 * (1.0 + t_)
        slope = cdf + (0.5 * GELU_C) * pre * (1.0 - t_ * t_) * (1.0 + (3.0 * GELU_A) * sq)
        act_t[:, rows] = (pre * cdf).astype(BF16)
        dpre_t[:, rows] = (back * slope).astype(BF16)
        return carry

    lax.fori_loop(0, tokens // size, chunk, 0)


def fetch(refs, dst, sem, cols=slice(None)):
    copies, at = [], 0
    for k, p in enumerate(refs):
        rows = pl.ds(at, p.shape[0])
        copies.append(pltpu.make_async_copy(p.at[:, cols], dst.at[rows, :], sem.at[k]))
        at += p.shape[0]
    for c in copies:
        c.start()
    for c in copies:
        c.wait()


def grads_kernel(n, first, features, hidden_scale, *refs):
    w, acc = refs[n], None if first else refs[n + 1]
    out, xg, act_t, dpre_t, sem = refs[-5:]
    fetch(refs[:n], xg, sem)
    hidden_both(xg, w, act_t, dpre_t, features, hidden_scale)
    for left, base in ((dpre_t, 0), (act_t, features)):

        def columns(j, carry, left=left, base=base):
            cols = pl.ds(pl.multiple_of(base + j * COLS, COLS), COLS)
            term = jnp.dot(left[...], xg[:, cols], preferred_element_type=F32)
            out[:, cols] = term if first else acc[:, cols] + term
            return carry

        lax.fori_loop(0, features // COLS, columns, 0)


ANY = pl.BlockSpec(memory_space=pl.ANY)
HBM = pl.BlockSpec(memory_space=pltpu.HBM)
VMEM = pl.BlockSpec(memory_space=pltpu.VMEM)


def resident(a):
    return pltpu.with_memory_space_constraint(a, pltpu.VMEM)


def accumulate(pieces, w, acc, hidden_scale):
    n = len(pieces)
    units, width = w.shape
    features = width // 2
    tokens = sum(p.shape[0] for p in pieces)
    first = acc is None
    return pl.pallas_call(
        functools.partial(grads_kernel, n, first, features, hidden_scale),
        in_specs=[HBM] * n + [VMEM] * (1 if first else 2),
        out_specs=VMEM,
        out_shape=pltpu.VMEM((units, width), F32),
        scratch_shapes=[
            pltpu.VMEM((tokens, width), BF16),
            pltpu.VMEM((units, tokens), BF16),
            pltpu.VMEM((units, tokens), BF16),
            pltpu.SemaphoreType.DMA((n,)),
        ],
        input_output_aliases={} if first else {n + 1: 0},
        compiler_params=pltpu.CompilerParams(vmem_limit_bytes=LIMIT),
        cost_estimate=pl.CostEstimate(
            flops=8 * tokens * units * features,
            bytes_accessed=tokens * width * 2,
            transcendentals=units * tokens,
        ),
        name="grads",
    )(*pieces, w, *(() if first else (acc,)))


def adam(total, scale, first, second, start):
    corr_one = 1.0 - BETA_ONE**STEP
    corr_two = 1.0 - BETA_TWO**STEP
    raw = total * scale
    first_new = (INNER_RATE * BETA_ONE / corr_one) * first.astype(F32) + (
        INNER_RATE * (1.0 - BETA_ONE) / corr_one
    ) * raw
    second_new = (BETA_TWO / corr_two) * second.astype(F32) + (
        (1.0 - BETA_TWO) / corr_two
    ) * (raw * raw)
    root = second_new * lax.rsqrt(second_new)
    return (first_new / (root + ADAM_EPS) + (INNER_RATE * DECAY) * start.astype(F32)).astype(BF16)


def pseudo_kernel(n, features, hidden_scale, *refs):
    where, pieces = refs[0], refs[1 : 1 + n]
    w, acc, m, v, keep, swap, far_keep, far_swap, total, act_t, dpre_t, xg, sem = refs[1 + n :]
    fetch(pieces, xg, sem)
    hidden_both(xg, w, act_t, dpre_t, features, hidden_scale)
    y, core = where[0], where[1]
    rows = w.shape[0] // SETS
    for half, left, scale in ((0, dpre_t, features ** (-0.5)), (1, act_t, hidden_scale)):

        def columns(j, carry, half=half, left=left, scale=scale):
            here = pl.ds(pl.multiple_of(j * COLS, COLS), COLS)
            cols = pl.ds(pl.multiple_of(half * features + j * COLS, COLS), COLS)
            total[...] = acc[:, cols] + jnp.dot(left[...], xg[:, cols], preferred_element_type=F32)

            def stepped(d, parity):
                chip = lax.rem(y + jnp.where(parity == 0, d, YS - d), YS)
                at = pl.ds(pl.multiple_of((2 * chip + parity) * rows, rows), rows)
                return adam(total[at, :], scale, m[at, cols], v[at, cols], w[at, cols])

            def ring(i, carry):
                for out, parity in ((keep, core), (swap, 1 - core)):
                    out[i, :, cols] = stepped(i + i // 2, parity)
                return carry

            lax.fori_loop(0, YS - 1, ring, carry)
            for out, parity in ((far_keep, core), (far_swap, 1 - core)):
                out[half, :, here] = stepped(2, parity)
            return carry

        lax.fori_loop(0, features // COLS, columns, 0)


def last_pseudo(where, pieces, w, acc, m, v, hidden_scale):
    n = len(pieces)
    units, width = w.shape
    features = width // 2
    rows = units // SETS
    tokens = sum(p.shape[0] for p in pieces)
    near = pltpu.VMEM((YS - 1, rows, width), BF16)
    far = pltpu.VMEM((2, rows, features), BF16)
    return pl.pallas_call(
        functools.partial(pseudo_kernel, n, features, hidden_scale),
        in_specs=[pl.BlockSpec(memory_space=pltpu.SMEM)] + [HBM] * n + [VMEM] * 4,
        out_specs=[VMEM] * 4,
        scratch_shapes=[
            pltpu.VMEM((units, COLS), F32),
            pltpu.VMEM((units, tokens), BF16),
            pltpu.VMEM((units, tokens), BF16),
            pltpu.VMEM((tokens, width), BF16),
            pltpu.SemaphoreType.DMA((n,)),
        ],
        out_shape=[near, near, far, far],
        compiler_params=pltpu.CompilerParams(vmem_limit_bytes=LIMIT),
        cost_estimate=pl.CostEstimate(
            flops=8 * features * tokens * units,
            bytes_accessed=units * width * 12 + tokens * width * 2,
            transcendentals=units * tokens,
        ),
        name="pseudo",
    )(where, *pieces, w, acc, m, v)


def home(info, d, parity):
    return 2 * lax.rem(info[0] + jnp.where(parity == 0, d, YS - d), YS) + parity


def run_copies(pairs, sem):
    copies = [pltpu.make_async_copy(a, b, sem.at[k]) for k, (a, b) in enumerate(pairs)]
    for c in copies:
        c.start()
    for c in copies:
        c.wait()


def near_own_kernel(info, own, nxt, prv, out, sem):
    run_copies(
        [(a.at[info[2 + d]], out.at[home(info, d, info[1])]) for a, d in ((own, 0), (nxt, 1), (prv, 3))],
        sem,
    )


def rest_kernel(info, near_own, near, own_l, own_r, other_l, other_r, begun, out, sem):
    half = own_l.shape[1]
    left, right = pl.ds(0, half), pl.ds(half, half)
    pairs = [
        (a, out.at[home(info, d, 1 - info[1])])
        for a, d in ((near_own, 0), (near.at[0], 1), (near.at[1], 3))
    ]
    for parity, l, r in ((info[1], own_l, own_r), (1 - info[1], other_l, other_r)):
        far = home(info, 2, parity)
        pairs += [(l, out.at[far, :, left]), (r, out.at[far, :, right])]
    run_copies(pairs, sem)


def assemble(kernel, info, pieces, begun, copies, rows, width):
    return pl.pallas_call(
        kernel,
        in_specs=[pl.BlockSpec(memory_space=pltpu.SMEM)]
        + [VMEM] * len(pieces)
        + [HBM] * len(begun),
        out_specs=HBM,
        out_shape=jax.ShapeDtypeStruct((SETS, rows, width), BF16),
        scratch_shapes=[pltpu.SemaphoreType.DMA((copies,))],
        input_output_aliases={1 + len(pieces): 0} if begun else {},
        cost_estimate=pl.CostEstimate(
            flops=0, bytes_accessed=SETS * rows * width * 2, transcendentals=0
        ),
        name=kernel.__name__,
    )(info, *pieces, *begun)


def per_device(
    input_activation_matrix,
    output_sensitivity,
    trajectory_initial_parameters,
    trajectory_gradient_average,
    trajectory_squared_average,
    common_expert_parameters,
    outer_inertia,
    trajectory_membership,
    punctual_flags,
):
    set_count, rows, width = trajectory_initial_parameters.shape[1:]
    units = set_count * rows
    features = width // 2
    hidden_scale = (SETS * UNIT) ** (-0.5)
    w = trajectory_initial_parameters[0].reshape(units, width)
    m = trajectory_gradient_average[0].reshape(units, width)
    v = trajectory_squared_average[0].reshape(units, width)

    me = lax.axis_index("path")
    y, core = me // 2, me % 2
    choices = common_expert_parameters.shape[1]
    eligible = jnp.arange(choices, dtype=jnp.int32)
    chosen = jnp.where(
        (trajectory_membership[:, :, None] == eligible[None, None, :])
        & (punctual_flags[:, None, None] == 1),
        1.0,
        0.0,
    ).astype(F32)
    turn = 1 - 2 * core
    chips = (y + turn * jnp.arange(YS, dtype=jnp.int32)) % YS
    sets = 2 * chips + core
    nxt_chip, prv_chip = chips[1], chips[3]
    mate = me ^ 1
    paths = jnp.stack(
        [me] * 4
        + [mate] * 4
        + [2 * prv_chip + core, 2 * prv_chip + 1 - core]
        + [2 * nxt_chip + core, 2 * nxt_chip + 1 - core]
    )
    at_sets = jnp.concatenate([sets, sets, sets[1:2], sets[1:2], sets[3:], sets[3:]])
    weights = chosen[paths, at_sets]
    pick_paths = jnp.concatenate([paths[:8], paths[10:], paths[8:10]])
    pick_sets = jnp.concatenate([sets, sets, sets[3:], sets[3:], sets[1:2], sets[1:2]])
    picks = trajectory_membership[pick_paths, pick_sets]
    tally = jnp.sum(chosen[:, me], axis=0)
    share = jnp.maximum(tally, 1.0)[:, None, None]
    where = jnp.stack([y, core]).astype(jnp.int32)
    info = jnp.concatenate([where, picks[:4]]).astype(jnp.int32)

    calls = (
        ((0, 0), (0, -1), (0, 1), (0, 2)),
        ((-1, 0), (1, 0), (-1, -1), (1, -1)),
        ((-1, 1), (1, 1), (-1, 2), (1, 2)),
        ((2, 0), (2, 1)),
    )
    seconds = {k: picks[k] == 1 for k in (4, 5, 7, 8, 9, 10, 11)}
    w, where, weights, seconds, share, info = lax.optimization_barrier(
        (w, where, weights, seconds, share, info)
    )
    w, m, v = resident(w), resident(m), resident(v)
    acc = None

    def compute(k, got):
        nonlocal acc
        acc = accumulate([got[b] for b in calls[k]], w, acc, hidden_scale)
        return acc

    got = gather_tokens(input_activation_matrix[0], output_sensitivity[0], compute)
    rest = [got[2, -1], got[2, 2]]

    common = common_expert_parameters[0]
    inertia = outer_inertia[0]

    def weighed(k, a):
        return weights[k][:, None, None] * a.astype(F32)[None]

    def exchange(swap, far_keep, far_swap):
        lefts = on_path(far_keep[0], 1), on_path(far_swap[0], -1, 1)
        rights = on_path(far_keep[1], -1), on_path(far_swap[1], 1, 1)
        return (on_path(swap, 0, 1), *lefts, *rights)

    keep, *outs = last_pseudo(where, rest, w, resident(acc), m, v, hidden_scale)
    mate_keep, l_same, l_cross, r_same, r_cross = exchange(*outs)

    def merged(i, d, lo=0, hi=width):
        return weighed(d, keep[i, :, lo:hi]) + weighed(4 + d, mate_keep[i, :, lo:hi])

    up_l = merged(1, 1, 0, features) + weighed(8, l_same) + weighed(9, l_cross)
    down_r = merged(2, 3, features) + weighed(10, r_same) + weighed(11, r_cross)
    up = jnp.concatenate([up_l.astype(BF16), merged(1, 1, features).astype(BF16)], -1)
    down = jnp.concatenate([merged(2, 3, 0, features).astype(BF16), down_r.astype(BF16)], -1)
    part_up, part_down = on_path(up, 1), on_path(down, -1)
    total = merged(0, 0) + part_up.astype(F32) + part_down.astype(F32)

    def refreshed(total):
        average = total / share
        new_inertia = INERTIA_FACTOR * inertia + average
        return common - GLOBAL_LEARNING * (average + INERTIA_FACTOR * new_inertia), new_inertia

    updated = refreshed(total)[0].astype(BF16)
    prv, nxt = on_path(updated, 1), on_path(updated, -1)
    new_experts, new_inertia = refreshed(after(total, prv, nxt))

    def picked(k, a, lo=0, hi=width):
        return jnp.where(seconds[k], a[1, :, lo:hi], a[0, :, lo:hi])

    own_l = on_path(picked(8, prv, 0, features), 1)
    other_l = on_path(picked(9, prv, 0, features), 1, 1)
    own_r = on_path(picked(10, nxt, features), -1)
    other_r = on_path(picked(11, nxt, features), -1, 1)
    near_own = on_path(picked(4, updated), 0, 1)
    near = on_path(jnp.stack([picked(5, nxt), picked(7, prv)]), 0, 1)
    returned = assemble(near_own_kernel, info, (updated, nxt, prv), (), 3, rows, width)
    far = (own_l, own_r, other_l, other_r)
    returned = assemble(rest_kernel, info, (near_own, near, *far), (returned,), 7, rows, width)
    return (new_experts[None], new_inertia[None], returned[None])


def solution(mesh):
    placed = (
        P("path", "fsdp", None),
        P("path", "fsdp", None),
        P("path", None, "fsdp", None),
        P("path", None, "fsdp", None),
        P("path", None, "fsdp", None),
        P("path", None, "fsdp", None),
        P("path", None, "fsdp", None),
        P(),
        P(),
    )
    return jax.shard_map(
        per_device,
        mesh=mesh,
        in_specs=placed,
        out_specs=(
            P("path", None, "fsdp", None),
            P("path", None, "fsdp", None),
            P("path", None, "fsdp", None),
        ),
        check_vma=False,
    )
```

```python
import functools

import jax
import jax.numpy as jnp
from jax import lax
from jax.experimental import pallas as pl
from jax.experimental.pallas import tpu as pltpu
from jax.sharding import PartitionSpec as P

UNIT = 1024
SETS = 8
STEP = 1000


BETA_ONE = 0.9
BETA_TWO = 0.999
ADAM_EPS = 1e-08
INNER_RATE = 0.05
DECAY = 0.1
GLOBAL_LEARNING = 0.7
INERTIA_FACTOR = 0.9

ZS, XS, YS = 4, 4, 4
GELU_C = 0.7978845608028654
GELU_A = 0.044715
NT = (((1,), (1,)), ((), ()))
F32 = jnp.float32
BF16 = jnp.bfloat16
COLS = 512
CHUNK = 256
LIMIT = 30 << 20


def plane_hop(da, db):
    pairs = []
    for p in range(2 * YS):
        dz, dx = (da, db) if p % 2 == 0 else (db, da)
        for z in range(ZS):
            for x in range(XS):
                to = ((z + dz) % ZS) * XS + (x + dx) % XS
                pairs.append((p * ZS * XS + z * XS + x, p * ZS * XS + to))
    return pairs


def path_hop(hop, flip):
    return [
        (i, ((i // 2 + (hop if i % 2 == 0 else -hop)) % YS) * 2 + ((i % 2) ^ flip))
        for i in range(2 * YS)
    ]


def on_path(a, hop, flip=0):
    return lax.ppermute(a, "path", path_hop(hop, flip))


def after(a, *others):
    return lax.optimization_barrier((a, *others))[0]


def gather_tokens(x, g, compute):
    def send(a, to, *others):
        if others:
            a = after(a, *others)
        return lax.ppermute(a, ("path", "fsdp"), plane_hop(*to))

    def join(x, g):
        return jnp.concatenate([x, g], 1)

    x_prv, g_nxt = send(x, (0, 1)), send(g, (0, -1))
    x_nxt, g_prv = send(x, (0, -1)), send(g, (0, 1))
    x_far, g_far = send(x_prv, (0, 1)), send(g_nxt, (0, -1))
    own = join(x, g)
    got = {(0, 0): own, (0, -1): join(x_prv, g_prv), (0, 1): join(x_nxt, g_nxt)}
    got[0, 2] = join(x_far, g_far)
    got[-1, 0] = send(own, (1, 0), x_prv, g_nxt)
    got[1, 0] = send(own, (-1, 0), x_prv, g_nxt)
    got[-1, -1] = send(got[0, -1], (1, 0), x_far, g_far)
    got[1, -1] = send(got[0, -1], (-1, 0), x_far, g_far)
    hold = {3: compute(0, got)}
    ups = [(-1, 0), (-1, -1), (-1, 1), (-1, 2), (2, 0), (2, -1)]
    downs = [(1, 0), (1, -1), (1, 1), (1, 2), (2, 1), (2, 2)]
    for j in range(2, 6):
        a, b = ups[j]
        c, d = downs[j]
        wait = [got[ups[j - 2]], got[downs[j - 2]]]
        if j == 4:
            hold[4] = compute(1, got)
        if j in hold:
            wait.append(hold[j])
        got[a, b] = send(got[0 if a == -1 else -1, b], (1, 0), *wait)
        got[c, d] = send(got[0 if c == 1 else 1, d], (-1, 0), *wait)
    compute(2, got)
    compute(3, got)
    return got


def hidden_both(xg, w, act_t, dpre_t, features, hidden_scale):
    in_scale = features ** (-0.5)
    tokens = xg.shape[0]
    size = CHUNK if tokens % CHUNK == 0 else tokens

    def chunk(t, carry):
        rows = pl.ds(pl.multiple_of(t * size, size), size)
        pre = (
            lax.dot_general(w[:, :features], xg[rows, :features], NT, preferred_element_type=F32)
            * in_scale
        )
        back = (
            lax.dot_general(w[:, features:], xg[rows, features:], NT, preferred_element_type=F32)
            * hidden_scale
        )
        sq = pre * pre
        t_ = jnp.tanh(GELU_C * pre * (1.0 + GELU_A * sq))
        cdf = 0.5 * (1.0 + t_)
        slope = cdf + (0.5 * GELU_C) * pre * (1.0 - t_ * t_) * (1.0 + (3.0 * GELU_A) * sq)
        act_t[:, rows] = (pre * cdf).astype(BF16)
        dpre_t[:, rows] = (back * slope).astype(BF16)
        return carry

    lax.fori_loop(0, tokens // size, chunk, 0)


def fetch(refs, dst, sem, cols=slice(None)):
    copies, at = [], 0
    for k, p in enumerate(refs):
        rows = pl.ds(at, p.shape[0])
        copies.append(pltpu.make_async_copy(p.at[:, cols], dst.at[rows, :], sem.at[k]))
        at += p.shape[0]
    for c in copies:
        c.start()
    for c in copies:
        c.wait()


def grads_kernel(n, first, features, hidden_scale, *refs):
    w, acc = refs[n], None if first else refs[n + 1]
    out, xg, act_t, dpre_t, sem = refs[-5:]
    fetch(refs[:n], xg, sem)
    hidden_both(xg, w, act_t, dpre_t, features, hidden_scale)
    for left, base in ((dpre_t, 0), (act_t, features)):

        def columns(j, carry, left=left, base=base):
            cols = pl.ds(pl.multiple_of(base + j * COLS, COLS), COLS)
            term = jnp.dot(left[...], xg[:, cols], preferred_element_type=F32)
            out[:, cols] = term if first else acc[:, cols] + term
            return carry

        lax.fori_loop(0, features // COLS, columns, 0)


ANY = pl.BlockSpec(memory_space=pl.ANY)
HBM = pl.BlockSpec(memory_space=pltpu.HBM)
VMEM = pl.BlockSpec(memory_space=pltpu.VMEM)


def resident(a):
    return pltpu.with_memory_space_constraint(a, pltpu.VMEM)


def accumulate(pieces, w, acc, hidden_scale):
    n = len(pieces)
    units, width = w.shape
    features = width // 2
    tokens = sum(p.shape[0] for p in pieces)
    first = acc is None
    return pl.pallas_call(
        functools.partial(grads_kernel, n, first, features, hidden_scale),
        in_specs=[HBM] * n + [VMEM] * (1 if first else 2),
        out_specs=VMEM,
        out_shape=pltpu.VMEM((units, width), F32),
        scratch_shapes=[
            pltpu.VMEM((tokens, width), BF16),
            pltpu.VMEM((units, tokens), BF16),
            pltpu.VMEM((units, tokens), BF16),
            pltpu.SemaphoreType.DMA((n,)),
        ],
        input_output_aliases={} if first else {n + 1: 0},
        compiler_params=pltpu.CompilerParams(vmem_limit_bytes=LIMIT),
        cost_estimate=pl.CostEstimate(
            flops=8 * tokens * units * features,
            bytes_accessed=tokens * width * 2,
            transcendentals=units * tokens,
        ),
        name="grads",
    )(*pieces, w, *(() if first else (acc,)))


def adam(total, scale, first, second, start):
    corr_one = 1.0 - BETA_ONE**STEP
    corr_two = 1.0 - BETA_TWO**STEP
    raw = total * scale
    first_new = (INNER_RATE * BETA_ONE / corr_one) * first.astype(F32) + (
        INNER_RATE * (1.0 - BETA_ONE) / corr_one
    ) * raw
    second_new = (BETA_TWO / corr_two) * second.astype(F32) + (
        (1.0 - BETA_TWO) / corr_two
    ) * (raw * raw)
    root = second_new * lax.rsqrt(second_new)
    return (first_new / (root + ADAM_EPS) + (INNER_RATE * DECAY) * start.astype(F32)).astype(BF16)


TAIL = (((2, 0), (2, 1)), ((0, 1), (1, 1), (3, 1)), ((0, 0), (1, 0), (3, 0)))


def pseudo_kernel(n, part, features, hidden_scale, *refs):
    where = refs[0]
    if part == 0:
        pieces = refs[1 : 1 + n]
        w, acc, m, v, out, xg, act_t, dpre_t, total, lines, sem = refs[1 + n :]
        fetch(pieces, xg, sem)
        hidden_both(xg, w, act_t, dpre_t, features, hidden_scale)
    else:
        w, acc, m, v, xg, act_t, dpre_t, out, total, lines = refs[1:]
    y, core = where[0], where[1]
    rows = w.shape[0] // SETS
    starts = []
    for d, other in TAIL[part]:
        parity = 1 - core if other else core
        chip = lax.rem(y + jnp.where(parity == 0, d, YS - d), YS)
        starts.append(pl.multiple_of((2 * chip + parity) * rows, rows))
    for half, left, scale in ((0, dpre_t, features ** (-0.5)), (1, act_t, hidden_scale)):
        for k, at in enumerate(starts):
            lines[k * rows : (k + 1) * rows, :] = left[pl.ds(at, rows), :]

        def columns(j, carry, half=half, scale=scale):
            cols = pl.ds(pl.multiple_of(half * features + j * COLS, COLS), COLS)
            total[...] = jnp.dot(lines[...], xg[:, cols], preferred_element_type=F32)
            for k, start in enumerate(starts):
                at = pl.ds(start, rows)
                grads = acc[at, cols] + total[k * rows : (k + 1) * rows, :]
                out[k, :, cols] = adam(grads, scale, m[at, cols], v[at, cols], w[at, cols])
            return carry

        lax.fori_loop(0, features // COLS, columns, 0)


def tail_pseudo(part, where, given, w, acc, m, v, hidden_scale):
    units, width = w.shape
    features = width // 2
    rows = units // SETS
    count = len(TAIL[part])
    tokens = sum(p.shape[0] for p in given) if part == 0 else given[0].shape[0]
    hid = pltpu.VMEM((units, tokens), BF16)
    kept = (w, acc, m, v)
    out_shape = [pltpu.VMEM((count, rows, width), BF16)]
    scratch = [pltpu.VMEM((count * rows, COLS), F32), pltpu.VMEM((count * rows, tokens), BF16)]
    if part == 0:
        operands, specs = (*given, *kept), [ANY] * len(given) + [VMEM] * 4
        out_shape += [pltpu.VMEM((tokens, width), BF16), hid, hid]
        scratch.append(pltpu.SemaphoreType.DMA((len(given),)))
    else:
        operands, specs = (*kept, *given), [VMEM] * 7
    return pl.pallas_call(
        functools.partial(pseudo_kernel, len(given), part, features, hidden_scale),
        in_specs=[pl.BlockSpec(memory_space=pltpu.SMEM)] + specs,
        out_specs=[VMEM] * len(out_shape),
        scratch_shapes=scratch,
        out_shape=out_shape,
        compiler_params=pltpu.CompilerParams(vmem_limit_bytes=LIMIT),
        cost_estimate=pl.CostEstimate(
            flops=4 * features * tokens * (rows * count + (units if part == 0 else 0)),
            bytes_accessed=rows * count * width * 12,
            transcendentals=rows * count * width,
        ),
        name="tail_%d" % part,
    )(where, *operands)


def home(info, d, parity):
    return 2 * lax.rem(info[0] + jnp.where(parity == 0, d, YS - d), YS) + parity


def run_copies(pairs, sem):
    copies = [pltpu.make_async_copy(a, b, sem.at[k]) for k, (a, b) in enumerate(pairs)]
    for c in copies:
        c.start()
    for c in copies:
        c.wait()


def near_own_kernel(info, own, nxt, prv, out, sem):
    run_copies(
        [(a.at[info[2 + d]], out.at[home(info, d, info[1])]) for a, d in ((own, 0), (nxt, 1), (prv, 3))],
        sem,
    )


def rest_kernel(info, near_own, near, own_l, own_r, other_l, other_r, begun, out, sem):
    half = own_l.shape[1]
    left, right = pl.ds(0, half), pl.ds(half, half)
    pairs = [
        (a, out.at[home(info, d, 1 - info[1])])
        for a, d in ((near_own, 0), (near.at[0], 1), (near.at[1], 3))
    ]
    for parity, l, r in ((info[1], own_l, own_r), (1 - info[1], other_l, other_r)):
        far = home(info, 2, parity)
        pairs += [(l, out.at[far, :, left]), (r, out.at[far, :, right])]
    run_copies(pairs, sem)


def assemble(kernel, info, pieces, begun, copies, rows, width):
    return pl.pallas_call(
        kernel,
        in_specs=[pl.BlockSpec(memory_space=pltpu.SMEM)]
        + [VMEM] * len(pieces)
        + [HBM] * len(begun),
        out_specs=HBM,
        out_shape=jax.ShapeDtypeStruct((SETS, rows, width), BF16),
        scratch_shapes=[pltpu.SemaphoreType.DMA((copies,))],
        input_output_aliases={1 + len(pieces): 0} if begun else {},
        cost_estimate=pl.CostEstimate(
            flops=0, bytes_accessed=SETS * rows * width * 2, transcendentals=0
        ),
        name=kernel.__name__,
    )(info, *pieces, *begun)


def per_device(
    input_activation_matrix,
    output_sensitivity,
    trajectory_initial_parameters,
    trajectory_gradient_average,
    trajectory_squared_average,
    common_expert_parameters,
    outer_inertia,
    trajectory_membership,
    punctual_flags,
):
    set_count, rows, width = trajectory_initial_parameters.shape[1:]
    units = set_count * rows
    features = width // 2
    hidden_scale = (SETS * UNIT) ** (-0.5)
    w = trajectory_initial_parameters[0].reshape(units, width)
    m = trajectory_gradient_average[0].reshape(units, width)
    v = trajectory_squared_average[0].reshape(units, width)

    me = lax.axis_index("path")
    y, core = me // 2, me % 2
    choices = common_expert_parameters.shape[1]
    eligible = jnp.arange(choices, dtype=jnp.int32)
    chosen = jnp.where(
        (trajectory_membership[:, :, None] == eligible[None, None, :])
        & (punctual_flags[:, None, None] == 1),
        1.0,
        0.0,
    ).astype(F32)
    turn = 1 - 2 * core
    chips = (y + turn * jnp.arange(YS, dtype=jnp.int32)) % YS
    sets = 2 * chips + core
    nxt_chip, prv_chip = chips[1], chips[3]
    mate = me ^ 1
    paths = jnp.stack(
        [me] * 4
        + [mate] * 4
        + [2 * prv_chip + core, 2 * prv_chip + 1 - core]
        + [2 * nxt_chip + core, 2 * nxt_chip + 1 - core]
    )
    at_sets = jnp.concatenate([sets, sets, sets[1:2], sets[1:2], sets[3:], sets[3:]])
    weights = chosen[paths, at_sets]
    pick_paths = jnp.concatenate([paths[:8], paths[10:], paths[8:10]])
    pick_sets = jnp.concatenate([sets, sets, sets[3:], sets[3:], sets[1:2], sets[1:2]])
    picks = trajectory_membership[pick_paths, pick_sets]
    tally = jnp.sum(chosen[:, me], axis=0)
    share = jnp.maximum(tally, 1.0)[:, None, None]
    where = jnp.stack([y, core]).astype(jnp.int32)
    info = jnp.concatenate([where, picks[:4]]).astype(jnp.int32)

    calls = (
        ((0, 0), (0, -1), (0, 1), (0, 2)),
        ((-1, 0), (1, 0), (-1, -1), (1, -1)),
        ((-1, 1), (1, 1), (-1, 2), (1, 2)),
        ((2, 0), (2, 1)),
    )
    seconds = {k: picks[k] == 1 for k in (4, 5, 7, 8, 9, 10, 11)}
    w, where, weights, seconds, share, info = lax.optimization_barrier(
        (w, where, weights, seconds, share, info)
    )
    w, m, v = resident(w), resident(m), resident(v)
    acc = None

    def compute(k, got):
        nonlocal acc
        acc = accumulate([got[b] for b in calls[k]], w, acc, hidden_scale)
        return acc

    got = gather_tokens(input_activation_matrix[0], output_sensitivity[0], compute)
    rest = [got[2, -1], got[2, 2]]

    common = common_expert_parameters[0]
    inertia = outer_inertia[0]

    def weighed(k, a):
        return weights[k][:, None, None] * a.astype(F32)[None]

    acc = resident(acc)
    far, *given = tail_pseudo(0, where, rest, w, acc, m, v, hidden_scale)
    given = [resident(a) for a in given]
    l_same, r_same = on_path(far[0, :, :features], 1), on_path(far[0, :, features:], -1)
    l_cross, r_cross = on_path(far[1, :, :features], -1, 1), on_path(far[1, :, features:], 1, 1)
    (swap,) = tail_pseudo(1, where, given, w, acc, m, v, hidden_scale)
    mate_keep = on_path(after(swap, l_same, r_same, l_cross, r_cross), 0, 1)
    (keep,) = tail_pseudo(2, after(where, swap), given, w, acc, m, v, hidden_scale)

    def merged(i, d, lo=0, hi=width):
        return weighed(d, keep[i, :, lo:hi]) + weighed(4 + d, mate_keep[i, :, lo:hi])

    up_l = merged(1, 1, 0, features) + weighed(8, l_same) + weighed(9, l_cross)
    down_r = merged(2, 3, features) + weighed(10, r_same) + weighed(11, r_cross)
    up = jnp.concatenate([up_l.astype(BF16), merged(1, 1, features).astype(BF16)], -1)
    down = jnp.concatenate([merged(2, 3, 0, features).astype(BF16), down_r.astype(BF16)], -1)
    part_up, part_down = on_path(up, 1), on_path(down, -1)
    total = merged(0, 0) + part_up.astype(F32) + part_down.astype(F32)

    def refreshed(total):
        average = total / share
        new_inertia = INERTIA_FACTOR * inertia + average
        return common - GLOBAL_LEARNING * (average + INERTIA_FACTOR * new_inertia), new_inertia

    updated = refreshed(total)[0].astype(BF16)
    prv, nxt = on_path(updated, 1), on_path(updated, -1)
    new_experts, new_inertia = refreshed(after(total, prv, nxt))

    def picked(k, a, lo=0, hi=width):
        return jnp.where(seconds[k], a[1, :, lo:hi], a[0, :, lo:hi])

    own_l = on_path(picked(8, prv, 0, features), 1)
    other_l = on_path(picked(9, prv, 0, features), 1, 1)
    own_r = on_path(picked(10, nxt, features), -1)
    other_r = on_path(picked(11, nxt, features), -1, 1)
    near_own = on_path(picked(4, updated), 0, 1)
    near = on_path(jnp.stack([picked(5, nxt), picked(7, prv)]), 0, 1)
    returned = assemble(near_own_kernel, info, (updated, nxt, prv), (), 3, rows, width)
    sent = [resident(a) for a in (near_own, near, own_l, own_r, other_l, other_r)]
    returned = assemble(rest_kernel, info, sent, (returned,), 7, rows, width)
    return (new_experts[None], new_inertia[None], returned[None])


def solution(mesh):
    placed = (
        P("path", "fsdp", None),
        P("path", "fsdp", None),
        P("path", None, "fsdp", None),
        P("path", None, "fsdp", None),
        P("path", None, "fsdp", None),
        P("path", None, "fsdp", None),
        P("path", None, "fsdp", None),
        P(),
        P(),
    )
    return jax.shard_map(
        per_device,
        mesh=mesh,
        in_specs=placed,
        out_specs=(
            P("path", None, "fsdp", None),
            P("path", None, "fsdp", None),
            P("path", None, "fsdp", None),
        ),
        check_vma=False,
    )
```

```python
import functools

import jax
import jax.numpy as jnp
from jax import lax
from jax.experimental import pallas as pl
from jax.experimental.pallas import tpu as pltpu
from jax.sharding import PartitionSpec as P

UNIT = 1024
SETS = 8
STEP = 1000


BETA_ONE = 0.9
BETA_TWO = 0.999
ADAM_EPS = 1e-08
INNER_RATE = 0.05
DECAY = 0.1
GLOBAL_LEARNING = 0.7
INERTIA_FACTOR = 0.9

ZS, XS, YS = 4, 4, 4
GELU_C = 0.7978845608028654
GELU_A = 0.044715
NT = (((1,), (1,)), ((), ()))
F32 = jnp.float32
BF16 = jnp.bfloat16
COLS = 512
CHUNK = 256
LIMIT = 24 << 20


def plane_hop(da, db):
    pairs = []
    for p in range(2 * YS):
        dz, dx = (da, db) if p % 2 == 0 else (db, da)
        for z in range(ZS):
            for x in range(XS):
                to = ((z + dz) % ZS) * XS + (x + dx) % XS
                pairs.append((p * ZS * XS + z * XS + x, p * ZS * XS + to))
    return pairs


def path_hop(hop, flip):
    return [
        (i, ((i // 2 + (hop if i % 2 == 0 else -hop)) % YS) * 2 + ((i % 2) ^ flip))
        for i in range(2 * YS)
    ]


def on_path(a, hop, flip=0):
    return lax.ppermute(a, "path", path_hop(hop, flip))


def after(a, *others):
    return lax.optimization_barrier((a, *others))[0]


def gather_tokens(x, g, compute):
    def send(a, to, *others):
        if others:
            a = after(a, *others)
        return lax.ppermute(a, ("path", "fsdp"), plane_hop(*to))

    def join(x, g):
        return jnp.concatenate([x, g], 1)

    x_prv, g_nxt = send(x, (0, 1)), send(g, (0, -1))
    x_nxt, g_prv = send(x, (0, -1)), send(g, (0, 1))
    x_far, g_far = send(x_prv, (0, 1)), send(g_nxt, (0, -1))
    own = join(x, g)
    got = {(0, 0): own, (0, -1): join(x_prv, g_prv), (0, 1): join(x_nxt, g_nxt)}
    got[0, 2] = join(x_far, g_far)
    got[-1, 0] = send(own, (1, 0), x_prv, g_nxt)
    got[1, 0] = send(own, (-1, 0), x_prv, g_nxt)
    got[-1, -1] = send(got[0, -1], (1, 0), x_far, g_far)
    got[1, -1] = send(got[0, -1], (-1, 0), x_far, g_far)
    hold = {3: compute(0, got)}
    ups = [(-1, 0), (-1, -1), (-1, 1), (-1, 2), (2, 0), (2, -1)]
    downs = [(1, 0), (1, -1), (1, 1), (1, 2), (2, 1), (2, 2)]
    for j in range(2, 6):
        a, b = ups[j]
        c, d = downs[j]
        wait = [got[ups[j - 2]], got[downs[j - 2]]]
        if j == 4:
            hold[4] = compute(1, got)
        if j in hold:
            wait.append(hold[j])
        got[a, b] = send(got[0 if a == -1 else -1, b], (1, 0), *wait)
        got[c, d] = send(got[0 if c == 1 else 1, d], (-1, 0), *wait)
    compute(2, got)
    compute(3, got)
    return got


def hidden_both(xg, w, act_t, dpre_t, features, hidden_scale):
    in_scale = features ** (-0.5)
    tokens = xg.shape[0]
    size = CHUNK if tokens % CHUNK == 0 else tokens

    def chunk(t, carry):
        rows = pl.ds(pl.multiple_of(t * size, size), size)
        pre = (
            lax.dot_general(w[:, :features], xg[rows, :features], NT, preferred_element_type=F32)
            * in_scale
        )
        back = (
            lax.dot_general(w[:, features:], xg[rows, features:], NT, preferred_element_type=F32)
            * hidden_scale
        )
        sq = pre * pre
        t_ = jnp.tanh(GELU_C * pre * (1.0 + GELU_A * sq))
        cdf = 0.5 * (1.0 + t_)
        slope = cdf + (0.5 * GELU_C) * pre * (1.0 - t_ * t_) * (1.0 + (3.0 * GELU_A) * sq)
        act_t[:, rows] = (pre * cdf).astype(BF16)
        dpre_t[:, rows] = (back * slope).astype(BF16)
        return carry

    lax.fori_loop(0, tokens // size, chunk, 0)


def fetch(refs, dst, sem, cols=slice(None)):
    copies, at = [], 0
    for k, p in enumerate(refs):
        rows = pl.ds(at, p.shape[0])
        copies.append(pltpu.make_async_copy(p.at[:, cols], dst.at[rows, :], sem.at[k]))
        at += p.shape[0]
    for c in copies:
        c.start()
    for c in copies:
        c.wait()


def grads_kernel(n, first, features, hidden_scale, *refs):
    w, acc = refs[n], None if first else refs[n + 1]
    out, xg, act_t, dpre_t, sem = refs[-5:]
    fetch(refs[:n], xg, sem)
    hidden_both(xg, w, act_t, dpre_t, features, hidden_scale)
    for left, base in ((dpre_t, 0), (act_t, features)):

        def columns(j, carry, left=left, base=base):
            cols = pl.ds(pl.multiple_of(base + j * COLS, COLS), COLS)
            term = jnp.dot(left[...], xg[:, cols], preferred_element_type=F32)
            out[:, cols] = term if first else acc[:, cols] + term
            return carry

        lax.fori_loop(0, features // COLS, columns, 0)


ANY = pl.BlockSpec(memory_space=pl.ANY)
HBM = pl.BlockSpec(memory_space=pltpu.HBM)
VMEM = pl.BlockSpec(memory_space=pltpu.VMEM)


def resident(a):
    return pltpu.with_memory_space_constraint(a, pltpu.VMEM)


def accumulate(pieces, w, acc, hidden_scale):
    n = len(pieces)
    units, width = w.shape
    features = width // 2
    tokens = sum(p.shape[0] for p in pieces)
    first = acc is None
    return pl.pallas_call(
        functools.partial(grads_kernel, n, first, features, hidden_scale),
        in_specs=[HBM] * n + [VMEM] * (1 if first else 2),
        out_specs=VMEM,
        out_shape=pltpu.VMEM((units, width), F32),
        scratch_shapes=[
            pltpu.VMEM((tokens, width), BF16),
            pltpu.VMEM((units, tokens), BF16),
            pltpu.VMEM((units, tokens), BF16),
            pltpu.SemaphoreType.DMA((n,)),
        ],
        input_output_aliases={} if first else {n + 1: 0},
        compiler_params=pltpu.CompilerParams(vmem_limit_bytes=LIMIT),
        cost_estimate=pl.CostEstimate(
            flops=8 * tokens * units * features,
            bytes_accessed=tokens * width * 2,
            transcendentals=units * tokens,
        ),
        name="grads",
    )(*pieces, w, *(() if first else (acc,)))


def adam(total, scale, first, second, start):
    corr_one = 1.0 - BETA_ONE**STEP
    corr_two = 1.0 - BETA_TWO**STEP
    raw = total * scale
    first_new = (INNER_RATE * BETA_ONE / corr_one) * first.astype(F32) + (
        INNER_RATE * (1.0 - BETA_ONE) / corr_one
    ) * raw
    second_new = (BETA_TWO / corr_two) * second.astype(F32) + (
        (1.0 - BETA_TWO) / corr_two
    ) * (raw * raw)
    root = second_new * lax.rsqrt(second_new)
    return (first_new / (root + ADAM_EPS) + (INNER_RATE * DECAY) * start.astype(F32)).astype(BF16)


TAIL = (((2, 0), (2, 1)), ((0, 1), (1, 1), (3, 1)), ((0, 0), (1, 0), (3, 0)))


def pseudo_kernel(n, part, features, hidden_scale, *refs):
    where = refs[0]
    if part == 0:
        pieces = refs[1 : 1 + n]
        w, acc, m, v, out, xg, act_t, dpre_t, total, lines, sem = refs[1 + n :]
        fetch(pieces, xg, sem)
        hidden_both(xg, w, act_t, dpre_t, features, hidden_scale)
    else:
        w, acc, m, v, xg, act_t, dpre_t, out, total, lines = refs[1:]
    y, core = where[0], where[1]
    rows = w.shape[0] // SETS
    starts = []
    for d, other in TAIL[part]:
        parity = 1 - core if other else core
        chip = lax.rem(y + jnp.where(parity == 0, d, YS - d), YS)
        starts.append(pl.multiple_of((2 * chip + parity) * rows, rows))
    for half, left, scale in ((0, dpre_t, features ** (-0.5)), (1, act_t, hidden_scale)):
        for k, at in enumerate(starts):
            lines[k * rows : (k + 1) * rows, :] = left[pl.ds(at, rows), :]

        def columns(j, carry, half=half, scale=scale):
            cols = pl.ds(pl.multiple_of(half * features + j * COLS, COLS), COLS)
            total[...] = jnp.dot(lines[...], xg[:, cols], preferred_element_type=F32)
            for k, start in enumerate(starts):
                at = pl.ds(start, rows)
                grads = acc[at, cols] + total[k * rows : (k + 1) * rows, :]
                out[k, :, cols] = adam(grads, scale, m[at, cols], v[at, cols], w[at, cols])
            return carry

        lax.fori_loop(0, features // COLS, columns, 0)


def tail_pseudo(part, where, given, w, acc, m, v, hidden_scale):
    units, width = w.shape
    features = width // 2
    rows = units // SETS
    count = len(TAIL[part])
    tokens = sum(p.shape[0] for p in given) if part == 0 else given[0].shape[0]
    hid = pltpu.VMEM((units, tokens), BF16)
    kept = (w, acc, m, v)
    out_shape = [pltpu.VMEM((count, rows, width), BF16)]
    scratch = [pltpu.VMEM((count * rows, COLS), F32), pltpu.VMEM((count * rows, tokens), BF16)]
    if part == 0:
        operands, specs = (*given, *kept), [ANY] * len(given) + [VMEM] * 4
        out_shape += [pltpu.VMEM((tokens, width), BF16), hid, hid]
        scratch.append(pltpu.SemaphoreType.DMA((len(given),)))
    else:
        operands, specs = (*kept, *given), [VMEM] * 7
    return pl.pallas_call(
        functools.partial(pseudo_kernel, len(given), part, features, hidden_scale),
        in_specs=[pl.BlockSpec(memory_space=pltpu.SMEM)] + specs,
        out_specs=[VMEM] * len(out_shape),
        scratch_shapes=scratch,
        out_shape=out_shape,
        compiler_params=pltpu.CompilerParams(vmem_limit_bytes=LIMIT),
        cost_estimate=pl.CostEstimate(
            flops=4 * features * tokens * (rows * count + (units if part == 0 else 0)),
            bytes_accessed=rows * count * width * 12,
            transcendentals=rows * count * width,
        ),
        name="tail_%d" % part,
    )(where, *operands)


def home(info, d, parity):
    return 2 * lax.rem(info[0] + jnp.where(parity == 0, d, YS - d), YS) + parity


def run_copies(pairs, sem):
    copies = [pltpu.make_async_copy(a, b, sem.at[k]) for k, (a, b) in enumerate(pairs)]
    for c in copies:
        c.start()
    for c in copies:
        c.wait()


def near_own_kernel(info, own, nxt, prv, out, sem):
    run_copies(
        [(a.at[info[2 + d]], out.at[home(info, d, info[1])]) for a, d in ((own, 0), (nxt, 1), (prv, 3))],
        sem,
    )


def rest_kernel(info, near_own, near, own_l, own_r, other_l, other_r, begun, out, sem):
    half = own_l.shape[1]
    left, right = pl.ds(0, half), pl.ds(half, half)
    pairs = [
        (a, out.at[home(info, d, 1 - info[1])])
        for a, d in ((near_own, 0), (near.at[0], 1), (near.at[1], 3))
    ]
    for parity, l, r in ((info[1], own_l, own_r), (1 - info[1], other_l, other_r)):
        far = home(info, 2, parity)
        pairs += [(l, out.at[far, :, left]), (r, out.at[far, :, right])]
    run_copies(pairs, sem)


def assemble(kernel, info, pieces, begun, copies, rows, width):
    return pl.pallas_call(
        kernel,
        in_specs=[pl.BlockSpec(memory_space=pltpu.SMEM)]
        + [VMEM] * len(pieces)
        + [HBM] * len(begun),
        out_specs=HBM,
        out_shape=jax.ShapeDtypeStruct((SETS, rows, width), BF16),
        scratch_shapes=[pltpu.SemaphoreType.DMA((copies,))],
        input_output_aliases={1 + len(pieces): 0} if begun else {},
        compiler_params=pltpu.CompilerParams(vmem_limit_bytes=8 << 20),
        cost_estimate=pl.CostEstimate(
            flops=0, bytes_accessed=SETS * rows * width * 2, transcendentals=0
        ),
        name=kernel.__name__,
    )(info, *pieces, *begun)


def per_device(
    input_activation_matrix,
    output_sensitivity,
    trajectory_initial_parameters,
    trajectory_gradient_average,
    trajectory_squared_average,
    common_expert_parameters,
    outer_inertia,
    trajectory_membership,
    punctual_flags,
):
    set_count, rows, width = trajectory_initial_parameters.shape[1:]
    units = set_count * rows
    features = width // 2
    hidden_scale = (SETS * UNIT) ** (-0.5)
    w = trajectory_initial_parameters[0].reshape(units, width)
    m = trajectory_gradient_average[0].reshape(units, width)
    v = trajectory_squared_average[0].reshape(units, width)

    me = lax.axis_index("path")
    y, core = me // 2, me % 2
    choices = common_expert_parameters.shape[1]
    eligible = jnp.arange(choices, dtype=jnp.int32)
    chosen = jnp.where(
        (trajectory_membership[:, :, None] == eligible[None, None, :])
        & (punctual_flags[:, None, None] == 1),
        1.0,
        0.0,
    ).astype(F32)
    turn = 1 - 2 * core
    chips = (y + turn * jnp.arange(YS, dtype=jnp.int32)) % YS
    sets = 2 * chips + core
    nxt_chip, prv_chip = chips[1], chips[3]
    mate = me ^ 1
    paths = jnp.stack(
        [me] * 4
        + [mate] * 4
        + [2 * prv_chip + core, 2 * prv_chip + 1 - core]
        + [2 * nxt_chip + core, 2 * nxt_chip + 1 - core]
    )
    at_sets = jnp.concatenate([sets, sets, sets[1:2], sets[1:2], sets[3:], sets[3:]])
    weights = chosen[paths, at_sets]
    pick_paths = jnp.concatenate([paths[:8], paths[10:], paths[8:10]])
    pick_sets = jnp.concatenate([sets, sets, sets[3:], sets[3:], sets[1:2], sets[1:2]])
    picks = trajectory_membership[pick_paths, pick_sets]
    tally = jnp.sum(chosen[:, me], axis=0)
    share = jnp.maximum(tally, 1.0)[:, None, None]
    where = jnp.stack([y, core]).astype(jnp.int32)
    info = jnp.concatenate([where, picks[:4]]).astype(jnp.int32)

    calls = (
        ((0, 0), (0, -1), (0, 1), (0, 2)),
        ((-1, 0), (1, 0), (-1, -1), (1, -1)),
        ((-1, 1), (1, 1), (-1, 2), (1, 2)),
        ((2, 0), (2, 1)),
    )
    seconds = {k: picks[k] == 1 for k in (4, 5, 7, 8, 9, 10, 11)}
    w, where, weights, seconds, share, info = lax.optimization_barrier(
        (w, where, weights, seconds, share, info)
    )
    w, m, v = resident(w), resident(m), resident(v)
    acc = None

    def compute(k, got):
        nonlocal acc
        acc = accumulate([got[b] for b in calls[k]], w, acc, hidden_scale)
        return acc

    got = gather_tokens(input_activation_matrix[0], output_sensitivity[0], compute)
    rest = [got[2, -1], got[2, 2]]

    common = common_expert_parameters[0]
    inertia = outer_inertia[0]

    def weighed(k, a):
        return weights[k][:, None, None] * a.astype(F32)[None]

    acc = resident(acc)
    far, *given = tail_pseudo(0, where, rest, w, acc, m, v, hidden_scale)
    given = [resident(a) for a in given]
    l_same, r_same = on_path(far[0, :, :features], 1), on_path(far[0, :, features:], -1)
    l_cross, r_cross = on_path(far[1, :, :features], -1, 1), on_path(far[1, :, features:], 1, 1)
    (swap,) = tail_pseudo(1, where, given, w, acc, m, v, hidden_scale)
    mate_keep = on_path(after(swap, l_same, r_same), 0, 1)
    (keep,) = tail_pseudo(2, after(where, swap), given, w, acc, m, v, hidden_scale)

    def merged(i, d, lo=0, hi=width):
        return weighed(d, keep[i, :, lo:hi]) + weighed(4 + d, mate_keep[i, :, lo:hi])

    up_l = merged(1, 1, 0, features) + weighed(8, l_same) + weighed(9, l_cross)
    down_r = merged(2, 3, features) + weighed(10, r_same) + weighed(11, r_cross)
    up = jnp.concatenate([up_l.astype(BF16), merged(1, 1, features).astype(BF16)], -1)
    down = jnp.concatenate([merged(2, 3, 0, features).astype(BF16), down_r.astype(BF16)], -1)
    part_up, part_down = on_path(up, 1), on_path(down, -1)
    total = merged(0, 0) + part_up.astype(F32) + part_down.astype(F32)

    def refreshed(total):
        average = total / share
        new_inertia = INERTIA_FACTOR * inertia + average
        return common - GLOBAL_LEARNING * (average + INERTIA_FACTOR * new_inertia), new_inertia

    updated = refreshed(total)[0].astype(BF16)
    prv, nxt = on_path(updated, 1), on_path(updated, -1)
    new_experts, new_inertia = refreshed(after(total, prv, nxt))

    def picked(k, a, lo=0, hi=width):
        return jnp.where(seconds[k], a[1, :, lo:hi], a[0, :, lo:hi])

    own_l = on_path(picked(8, prv, 0, features), 1)
    other_l = on_path(picked(9, prv, 0, features), 1, 1)
    own_r = on_path(picked(10, nxt, features), -1)
    other_r = on_path(picked(11, nxt, features), -1, 1)
    near_own = on_path(picked(4, updated), 0, 1)
    near = on_path(jnp.stack([picked(5, nxt), picked(7, prv)]), 0, 1)
    returned = assemble(near_own_kernel, info, [resident(a) for a in (updated, nxt, prv)], (), 3, rows, width)
    sent = [resident(a) for a in (near_own, near, own_l, own_r, other_l, other_r)]
    returned = assemble(rest_kernel, info, sent, (returned,), 7, rows, width)
    return (new_experts[None], new_inertia[None], returned[None])


def solution(mesh):
    placed = (
        P("path", "fsdp", None),
        P("path", "fsdp", None),
        P("path", None, "fsdp", None),
        P("path", None, "fsdp", None),
        P("path", None, "fsdp", None),
        P("path", None, "fsdp", None),
        P("path", None, "fsdp", None),
        P(),
        P(),
    )
    return jax.shard_map(
        per_device,
        mesh=mesh,
        in_specs=placed,
        out_specs=(
            P("path", None, "fsdp", None),
            P("path", None, "fsdp", None),
            P("path", None, "fsdp", None),
        ),
        check_vma=False,
    )
```

```python
import functools

import jax
import jax.numpy as jnp
from jax import lax
from jax.experimental import pallas as pl
from jax.experimental.pallas import tpu as pltpu
from jax.sharding import PartitionSpec as P

UNIT = 1024
SETS = 8
STEP = 1000


BETA_ONE = 0.9
BETA_TWO = 0.999
ADAM_EPS = 1e-08
INNER_RATE = 0.05
DECAY = 0.1
GLOBAL_LEARNING = 0.7
INERTIA_FACTOR = 0.9

ZS, XS, YS = 4, 4, 4
GELU_C = 0.7978845608028654
GELU_A = 0.044715
NT = (((1,), (1,)), ((), ()))
F32 = jnp.float32
BF16 = jnp.bfloat16
COLS = 512
CHUNK = 256
LIMIT = 24 << 20


def plane_hop(da, db):
    pairs = []
    for p in range(2 * YS):
        dz, dx = (da, db) if p % 2 == 0 else (db, da)
        for z in range(ZS):
            for x in range(XS):
                to = ((z + dz) % ZS) * XS + (x + dx) % XS
                pairs.append((p * ZS * XS + z * XS + x, p * ZS * XS + to))
    return pairs


def path_hop(hop, flip):
    return [
        (i, ((i // 2 + (hop if i % 2 == 0 else -hop)) % YS) * 2 + ((i % 2) ^ flip))
        for i in range(2 * YS)
    ]


def on_path(a, hop, flip=0):
    return lax.ppermute(a, "path", path_hop(hop, flip))


def after(a, *others):
    return lax.optimization_barrier((a, *others))[0]


def gather_tokens(x, g, compute):
    def send(a, to, *others):
        if others:
            a = after(a, *others)
        return lax.ppermute(a, ("path", "fsdp"), plane_hop(*to))

    def join(x, g):
        return jnp.concatenate([x, g], 1)

    x_prv, g_nxt = send(x, (0, 1)), send(g, (0, -1))
    x_nxt, g_prv = send(x, (0, -1), x_prv, g_nxt), send(g, (0, 1), x_prv, g_nxt)
    x_far, g_far = send(x_prv, (0, 1)), send(g_nxt, (0, -1))
    own = join(x, g)
    got = {(0, 0): own, (0, -1): join(x_prv, g_prv), (0, 1): join(x_nxt, g_nxt)}
    got[0, 2] = join(x_far, g_far)
    got[-1, 0], got[1, 0] = send(own, (1, 0)), send(own, (-1, 0))
    got[-1, -1] = send(got[0, -1], (1, 0), x_far, g_far)
    got[1, -1] = send(got[0, -1], (-1, 0), x_far, g_far)
    hold = {3: compute(0, got)}
    ups = [(-1, 0), (-1, -1), (-1, 1), (-1, 2), (2, 0), (2, -1)]
    downs = [(1, 0), (1, -1), (1, 1), (1, 2), (2, 1), (2, 2)]
    for j in range(2, 6):
        a, b = ups[j]
        c, d = downs[j]
        wait = [got[ups[j - 2]], got[downs[j - 2]]]
        if j == 4:
            hold[4] = compute(1, got)
        if j in hold:
            wait.append(hold[j])
        got[a, b] = send(got[0 if a == -1 else -1, b], (1, 0), *wait)
        got[c, d] = send(got[0 if c == 1 else 1, d], (-1, 0), *wait)
    compute(2, got)
    compute(3, got)
    return got


def hidden_both(xg, w, act_t, dpre_t, features, hidden_scale):
    in_scale = features ** (-0.5)
    tokens = xg.shape[0]
    size = CHUNK if tokens % CHUNK == 0 else tokens

    def chunk(t, carry):
        rows = pl.ds(pl.multiple_of(t * size, size), size)
        pre = (
            lax.dot_general(w[:, :features], xg[rows, :features], NT, preferred_element_type=F32)
            * in_scale
        )
        back = (
            lax.dot_general(w[:, features:], xg[rows, features:], NT, preferred_element_type=F32)
            * hidden_scale
        )
        sq = pre * pre
        t_ = jnp.tanh(GELU_C * pre * (1.0 + GELU_A * sq))
        cdf = 0.5 * (1.0 + t_)
        slope = cdf + (0.5 * GELU_C) * pre * (1.0 - t_ * t_) * (1.0 + (3.0 * GELU_A) * sq)
        act_t[:, rows] = (pre * cdf).astype(BF16)
        dpre_t[:, rows] = (back * slope).astype(BF16)
        return carry

    lax.fori_loop(0, tokens // size, chunk, 0)


def fetch(refs, dst, sem, cols=slice(None)):
    copies, at = [], 0
    for k, p in enumerate(refs):
        rows = pl.ds(at, p.shape[0])
        copies.append(pltpu.make_async_copy(p.at[:, cols], dst.at[rows, :], sem.at[k]))
        at += p.shape[0]
    for c in copies:
        c.start()
    for c in copies:
        c.wait()


def grads_kernel(n, first, features, hidden_scale, *refs):
    w, acc = refs[n], None if first else refs[n + 1]
    out, xg, act_t, dpre_t, sem = refs[-5:]
    fetch(refs[:n], xg, sem)
    hidden_both(xg, w, act_t, dpre_t, features, hidden_scale)
    for left, base in ((dpre_t, 0), (act_t, features)):

        def columns(j, carry, left=left, base=base):
            cols = pl.ds(pl.multiple_of(base + j * COLS, COLS), COLS)
            term = jnp.dot(left[...], xg[:, cols], preferred_element_type=F32)
            out[:, cols] = term if first else acc[:, cols] + term
            return carry

        lax.fori_loop(0, features // COLS, columns, 0)


ANY = pl.BlockSpec(memory_space=pl.ANY)
HBM = pl.BlockSpec(memory_space=pltpu.HBM)
VMEM = pl.BlockSpec(memory_space=pltpu.VMEM)


def resident(a):
    return pltpu.with_memory_space_constraint(a, pltpu.VMEM)


def accumulate(pieces, w, acc, hidden_scale):
    n = len(pieces)
    units, width = w.shape
    features = width // 2
    tokens = sum(p.shape[0] for p in pieces)
    first = acc is None
    return pl.pallas_call(
        functools.partial(grads_kernel, n, first, features, hidden_scale),
        in_specs=[HBM] * n + [VMEM] * (1 if first else 2),
        out_specs=VMEM,
        out_shape=pltpu.VMEM((units, width), F32),
        scratch_shapes=[
            pltpu.VMEM((tokens, width), BF16),
            pltpu.VMEM((units, tokens), BF16),
            pltpu.VMEM((units, tokens), BF16),
            pltpu.SemaphoreType.DMA((n,)),
        ],
        input_output_aliases={} if first else {n + 1: 0},
        compiler_params=pltpu.CompilerParams(vmem_limit_bytes=LIMIT),
        cost_estimate=pl.CostEstimate(
            flops=8 * tokens * units * features,
            bytes_accessed=tokens * width * 2,
            transcendentals=units * tokens,
        ),
        name="grads",
    )(*pieces, w, *(() if first else (acc,)))


def adam(total, scale, first, second, start):
    corr_one = 1.0 - BETA_ONE**STEP
    corr_two = 1.0 - BETA_TWO**STEP
    raw = total * scale
    first_new = (INNER_RATE * BETA_ONE / corr_one) * first.astype(F32) + (
        INNER_RATE * (1.0 - BETA_ONE) / corr_one
    ) * raw
    second_new = (BETA_TWO / corr_two) * second.astype(F32) + (
        (1.0 - BETA_TWO) / corr_two
    ) * (raw * raw)
    root = second_new * lax.rsqrt(second_new)
    return (first_new / (root + ADAM_EPS) + (INNER_RATE * DECAY) * start.astype(F32)).astype(BF16)


TAIL = (((2, 0), (2, 1)), ((0, 1), (1, 1), (3, 1)), ((0, 0), (1, 0), (3, 0)))


def pseudo_kernel(n, part, features, hidden_scale, *refs):
    where = refs[0]
    if part == 0:
        pieces = refs[1 : 1 + n]
        w, acc, m, v, out, xg, act_t, dpre_t, total, lines, sem = refs[1 + n :]
        fetch(pieces, xg, sem)
        hidden_both(xg, w, act_t, dpre_t, features, hidden_scale)
    else:
        w, acc, m, v, xg, act_t, dpre_t, out, total, lines = refs[1:]
    y, core = where[0], where[1]
    rows = w.shape[0] // SETS
    starts = []
    for d, other in TAIL[part]:
        parity = 1 - core if other else core
        chip = lax.rem(y + jnp.where(parity == 0, d, YS - d), YS)
        starts.append(pl.multiple_of((2 * chip + parity) * rows, rows))
    for half, left, scale in ((0, dpre_t, features ** (-0.5)), (1, act_t, hidden_scale)):
        for k, at in enumerate(starts):
            lines[k * rows : (k + 1) * rows, :] = left[pl.ds(at, rows), :]

        def columns(j, carry, half=half, scale=scale):
            cols = pl.ds(pl.multiple_of(half * features + j * COLS, COLS), COLS)
            total[...] = jnp.dot(lines[...], xg[:, cols], preferred_element_type=F32)
            for k, start in enumerate(starts):
                at = pl.ds(start, rows)
                grads = acc[at, cols] + total[k * rows : (k + 1) * rows, :]
                out[k, :, cols] = adam(grads, scale, m[at, cols], v[at, cols], w[at, cols])
            return carry

        lax.fori_loop(0, features // COLS, columns, 0)


def tail_pseudo(part, where, given, w, acc, m, v, hidden_scale):
    units, width = w.shape
    features = width // 2
    rows = units // SETS
    count = len(TAIL[part])
    tokens = sum(p.shape[0] for p in given) if part == 0 else given[0].shape[0]
    hid = pltpu.VMEM((units, tokens), BF16)
    kept = (w, acc, m, v)
    out_shape = [pltpu.VMEM((count, rows, width), BF16)]
    scratch = [pltpu.VMEM((count * rows, COLS), F32), pltpu.VMEM((count * rows, tokens), BF16)]
    if part == 0:
        operands, specs = (*given, *kept), [ANY] * len(given) + [VMEM] * 4
        out_shape += [pltpu.VMEM((tokens, width), BF16), hid, hid]
        scratch.append(pltpu.SemaphoreType.DMA((len(given),)))
    else:
        operands, specs = (*kept, *given), [VMEM] * 7
    return pl.pallas_call(
        functools.partial(pseudo_kernel, len(given), part, features, hidden_scale),
        in_specs=[pl.BlockSpec(memory_space=pltpu.SMEM)] + specs,
        out_specs=[VMEM] * len(out_shape),
        scratch_shapes=scratch,
        out_shape=out_shape,
        compiler_params=pltpu.CompilerParams(vmem_limit_bytes=LIMIT),
        cost_estimate=pl.CostEstimate(
            flops=4 * features * tokens * (rows * count + (units if part == 0 else 0)),
            bytes_accessed=rows * count * width * 12,
            transcendentals=rows * count * width,
        ),
        name="tail_%d" % part,
    )(where, *operands)


def home(info, d, parity):
    return 2 * lax.rem(info[0] + jnp.where(parity == 0, d, YS - d), YS) + parity


def run_copies(pairs, sem):
    copies = [pltpu.make_async_copy(a, b, sem.at[k]) for k, (a, b) in enumerate(pairs)]
    for c in copies:
        c.start()
    for c in copies:
        c.wait()


def near_own_kernel(info, own, nxt, prv, out, sem):
    run_copies(
        [(a.at[info[2 + d]], out.at[home(info, d, info[1])]) for a, d in ((own, 0), (nxt, 1), (prv, 3))],
        sem,
    )


def rest_kernel(info, near_own, near, own_l, own_r, other_l, other_r, begun, out, sem):
    half = own_l.shape[1]
    left, right = pl.ds(0, half), pl.ds(half, half)
    pairs = [
        (a, out.at[home(info, d, 1 - info[1])])
        for a, d in ((near_own, 0), (near.at[0], 1), (near.at[1], 3))
    ]
    for parity, l, r in ((info[1], own_l, own_r), (1 - info[1], other_l, other_r)):
        far = home(info, 2, parity)
        pairs += [(l, out.at[far, :, left]), (r, out.at[far, :, right])]
    run_copies(pairs, sem)


def assemble(kernel, info, pieces, begun, copies, rows, width):
    return pl.pallas_call(
        kernel,
        in_specs=[pl.BlockSpec(memory_space=pltpu.SMEM)]
        + [VMEM] * len(pieces)
        + [HBM] * len(begun),
        out_specs=HBM,
        out_shape=jax.ShapeDtypeStruct((SETS, rows, width), BF16),
        scratch_shapes=[pltpu.SemaphoreType.DMA((copies,))],
        input_output_aliases={1 + len(pieces): 0} if begun else {},
        compiler_params=pltpu.CompilerParams(vmem_limit_bytes=8 << 20),
        cost_estimate=pl.CostEstimate(
            flops=0, bytes_accessed=SETS * rows * width * 2, transcendentals=0
        ),
        name=kernel.__name__,
    )(info, *pieces, *begun)


def per_device(
    input_activation_matrix,
    output_sensitivity,
    trajectory_initial_parameters,
    trajectory_gradient_average,
    trajectory_squared_average,
    common_expert_parameters,
    outer_inertia,
    trajectory_membership,
    punctual_flags,
):
    set_count, rows, width = trajectory_initial_parameters.shape[1:]
    units = set_count * rows
    features = width // 2
    hidden_scale = (SETS * UNIT) ** (-0.5)
    w = trajectory_initial_parameters[0].reshape(units, width)
    m = trajectory_gradient_average[0].reshape(units, width)
    v = trajectory_squared_average[0].reshape(units, width)

    me = lax.axis_index("path")
    y, core = me // 2, me % 2
    choices = common_expert_parameters.shape[1]
    eligible = jnp.arange(choices, dtype=jnp.int32)
    chosen = jnp.where(
        (trajectory_membership[:, :, None] == eligible[None, None, :])
        & (punctual_flags[:, None, None] == 1),
        1.0,
        0.0,
    ).astype(F32)
    turn = 1 - 2 * core
    chips = (y + turn * jnp.arange(YS, dtype=jnp.int32)) % YS
    sets = 2 * chips + core
    nxt_chip, prv_chip = chips[1], chips[3]
    mate = me ^ 1
    paths = jnp.stack(
        [me] * 4
        + [mate] * 4
        + [2 * prv_chip + core, 2 * prv_chip + 1 - core]
        + [2 * nxt_chip + core, 2 * nxt_chip + 1 - core]
    )
    at_sets = jnp.concatenate([sets, sets, sets[1:2], sets[1:2], sets[3:], sets[3:]])
    weights = chosen[paths, at_sets]
    pick_paths = jnp.concatenate([paths[:8], paths[10:], paths[8:10]])
    pick_sets = jnp.concatenate([sets, sets, sets[3:], sets[3:], sets[1:2], sets[1:2]])
    picks = trajectory_membership[pick_paths, pick_sets]
    tally = jnp.sum(chosen[:, me], axis=0)
    share = jnp.maximum(tally, 1.0)[:, None, None]
    where = jnp.stack([y, core]).astype(jnp.int32)
    info = jnp.concatenate([where, picks[:4]]).astype(jnp.int32)

    calls = (
        ((0, 0), (0, -1), (0, 1), (0, 2)),
        ((-1, 0), (1, 0), (-1, -1), (1, -1)),
        ((-1, 1), (1, 1), (-1, 2), (1, 2)),
        ((2, 0), (2, 1)),
    )
    seconds = {k: picks[k] == 1 for k in (4, 5, 7, 8, 9, 10, 11)}
    w, where, weights, seconds, share, info = lax.optimization_barrier(
        (w, where, weights, seconds, share, info)
    )
    w, m, v = resident(w), resident(m), resident(v)
    acc = None

    def compute(k, got):
        nonlocal acc
        acc = accumulate([got[b] for b in calls[k]], w, acc, hidden_scale)
        return acc

    got = gather_tokens(input_activation_matrix[0], output_sensitivity[0], compute)
    rest = [got[2, -1], got[2, 2]]

    common = common_expert_parameters[0]
    inertia = outer_inertia[0]

    def weighed(k, a):
        return weights[k][:, None, None] * a.astype(F32)[None]

    acc = resident(acc)
    far, *given = tail_pseudo(0, where, rest, w, acc, m, v, hidden_scale)
    given = [resident(a) for a in given]
    l_same, r_same = on_path(far[0, :, :features], 1), on_path(far[0, :, features:], -1)
    l_cross, r_cross = on_path(far[1, :, :features], -1, 1), on_path(far[1, :, features:], 1, 1)
    (swap,) = tail_pseudo(1, where, given, w, acc, m, v, hidden_scale)
    mate_keep = on_path(after(swap, l_same, r_same), 0, 1)
    (keep,) = tail_pseudo(2, after(where, swap), given, w, acc, m, v, hidden_scale)

    def merged(i, d, lo=0, hi=width):
        return weighed(d, keep[i, :, lo:hi]) + weighed(4 + d, mate_keep[i, :, lo:hi])

    up_l = merged(1, 1, 0, features) + weighed(8, l_same) + weighed(9, l_cross)
    down_r = merged(2, 3, features) + weighed(10, r_same) + weighed(11, r_cross)
    up = jnp.concatenate([up_l.astype(BF16), merged(1, 1, features).astype(BF16)], -1)
    down = jnp.concatenate([merged(2, 3, 0, features).astype(BF16), down_r.astype(BF16)], -1)
    part_up, part_down = on_path(up, 1), on_path(down, -1)
    total = merged(0, 0) + part_up.astype(F32) + part_down.astype(F32)

    def refreshed(total):
        average = total / share
        new_inertia = INERTIA_FACTOR * inertia + average
        return common - GLOBAL_LEARNING * (average + INERTIA_FACTOR * new_inertia), new_inertia

    updated = refreshed(total)[0].astype(BF16)
    prv, nxt = on_path(updated, 1), on_path(updated, -1)
    new_experts, new_inertia = refreshed(after(total, prv, nxt))

    def picked(k, a, lo=0, hi=width):
        return jnp.where(seconds[k], a[1, :, lo:hi], a[0, :, lo:hi])

    own_l = on_path(picked(8, prv, 0, features), 1)
    other_l = on_path(picked(9, prv, 0, features), 1, 1)
    own_r = on_path(picked(10, nxt, features), -1)
    other_r = on_path(picked(11, nxt, features), -1, 1)
    near_own = on_path(picked(4, updated), 0, 1)
    near = on_path(jnp.stack([picked(5, nxt), picked(7, prv)]), 0, 1)
    returned = assemble(near_own_kernel, info, [resident(a) for a in (updated, nxt, prv)], (), 3, rows, width)
    sent = [resident(a) for a in (near_own, near, own_l, own_r, other_l, other_r)]
    returned = assemble(rest_kernel, info, sent, (returned,), 7, rows, width)
    return (new_experts[None], new_inertia[None], returned[None])


def solution(mesh):
    placed = (
        P("path", "fsdp", None),
        P("path", "fsdp", None),
        P("path", None, "fsdp", None),
        P("path", None, "fsdp", None),
        P("path", None, "fsdp", None),
        P("path", None, "fsdp", None),
        P("path", None, "fsdp", None),
        P(),
        P(),
    )
    return jax.shard_map(
        per_device,
        mesh=mesh,
        in_specs=placed,
        out_specs=(
            P("path", None, "fsdp", None),
            P("path", None, "fsdp", None),
            P("path", None, "fsdp", None),
        ),
        check_vma=False,
    )
```

```python
import functools

import jax
import jax.numpy as jnp
from jax import lax
from jax.experimental import pallas as pl
from jax.experimental.pallas import tpu as pltpu
from jax.sharding import PartitionSpec as P

UNIT = 1024
SETS = 8
STEP = 1000


BETA_ONE = 0.9
BETA_TWO = 0.999
ADAM_EPS = 1e-08
INNER_RATE = 0.05
DECAY = 0.1
GLOBAL_LEARNING = 0.7
INERTIA_FACTOR = 0.9

ZS, XS, YS = 4, 4, 4
GELU_C = 0.7978845608028654
GELU_A = 0.044715
NT = (((1,), (1,)), ((), ()))
F32 = jnp.float32
BF16 = jnp.bfloat16
COLS = 512
CHUNK = 256
LIMIT = 24 << 20


def plane_hop(da, db):
    pairs = []
    for p in range(2 * YS):
        dz, dx = (da, db) if p % 2 == 0 else (db, da)
        for z in range(ZS):
            for x in range(XS):
                to = ((z + dz) % ZS) * XS + (x + dx) % XS
                pairs.append((p * ZS * XS + z * XS + x, p * ZS * XS + to))
    return pairs


def path_hop(hop, flip):
    return [
        (i, ((i // 2 + (hop if i % 2 == 0 else -hop)) % YS) * 2 + ((i % 2) ^ flip))
        for i in range(2 * YS)
    ]


def on_path(a, hop, flip=0):
    return lax.ppermute(a, "path", path_hop(hop, flip))


def after(a, *others):
    return lax.optimization_barrier((a, *others))[0]


def gather_tokens(x, g, compute):
    def send(a, to, *others):
        if others:
            a = after(a, *others)
        return lax.ppermute(a, ("path", "fsdp"), plane_hop(*to))

    def join(x, g):
        return jnp.concatenate([x, g], 1)

    x_prv, g_nxt = send(x, (0, 1)), send(g, (0, -1))
    x_nxt, g_prv = send(x, (0, -1), x_prv, g_nxt), send(g, (0, 1), x_prv, g_nxt)
    x_far, g_far = send(x_prv, (0, 1)), send(g_nxt, (0, -1))
    own = join(x, g)
    got = {(0, 0): own, (0, -1): join(x_prv, g_prv), (0, 1): join(x_nxt, g_nxt)}
    got[0, 2] = join(x_far, g_far)
    got[-1, 0], got[1, 0] = send(own, (1, 0)), send(own, (-1, 0))
    got[-1, -1], got[1, -1] = send(got[0, -1], (1, 0)), send(got[0, -1], (-1, 0))
    hold = {3: compute(0, got)}
    ups = [(-1, 0), (-1, -1), (-1, 1), (-1, 2), (2, 0), (2, -1)]
    downs = [(1, 0), (1, -1), (1, 1), (1, 2), (2, 1), (2, 2)]
    for j in range(2, 6):
        a, b = ups[j]
        c, d = downs[j]
        wait = [got[ups[j - 2]], got[downs[j - 2]]]
        if j == 4:
            hold[4] = compute(1, got)
        if j in hold:
            wait.append(hold[j])
        got[a, b] = send(got[0 if a == -1 else -1, b], (1, 0), *wait)
        got[c, d] = send(got[0 if c == 1 else 1, d], (-1, 0), *wait)
    compute(2, got)
    compute(3, got)
    return got


def hidden_both(xg, w, act_t, dpre_t, features, hidden_scale):
    in_scale = features ** (-0.5)
    tokens = xg.shape[0]
    size = CHUNK if tokens % CHUNK == 0 else tokens

    def chunk(t, carry):
        rows = pl.ds(pl.multiple_of(t * size, size), size)
        pre = (
            lax.dot_general(w[:, :features], xg[rows, :features], NT, preferred_element_type=F32)
            * in_scale
        )
        back = (
            lax.dot_general(w[:, features:], xg[rows, features:], NT, preferred_element_type=F32)
            * hidden_scale
        )
        sq = pre * pre
        t_ = jnp.tanh(GELU_C * pre * (1.0 + GELU_A * sq))
        cdf = 0.5 * (1.0 + t_)
        slope = cdf + (0.5 * GELU_C) * pre * (1.0 - t_ * t_) * (1.0 + (3.0 * GELU_A) * sq)
        act_t[:, rows] = (pre * cdf).astype(BF16)
        dpre_t[:, rows] = (back * slope).astype(BF16)
        return carry

    lax.fori_loop(0, tokens // size, chunk, 0)


def fetch(refs, dst, sem, cols=slice(None)):
    copies, at = [], 0
    for k, p in enumerate(refs):
        rows = pl.ds(at, p.shape[0])
        copies.append(pltpu.make_async_copy(p.at[:, cols], dst.at[rows, :], sem.at[k]))
        at += p.shape[0]
    for c in copies:
        c.start()
    for c in copies:
        c.wait()


def grads_kernel(n, first, features, hidden_scale, *refs):
    w, acc = refs[n], None if first else refs[n + 1]
    out, xg, act_t, dpre_t, sem = refs[-5:]
    fetch(refs[:n], xg, sem)
    hidden_both(xg, w, act_t, dpre_t, features, hidden_scale)
    for left, base in ((dpre_t, 0), (act_t, features)):

        def columns(j, carry, left=left, base=base):
            cols = pl.ds(pl.multiple_of(base + j * COLS, COLS), COLS)
            term = jnp.dot(left[...], xg[:, cols], preferred_element_type=F32)
            out[:, cols] = term if first else acc[:, cols] + term
            return carry

        lax.fori_loop(0, features // COLS, columns, 0)


ANY = pl.BlockSpec(memory_space=pl.ANY)
HBM = pl.BlockSpec(memory_space=pltpu.HBM)
VMEM = pl.BlockSpec(memory_space=pltpu.VMEM)


def resident(a):
    return pltpu.with_memory_space_constraint(a, pltpu.VMEM)


def accumulate(pieces, w, acc, hidden_scale):
    n = len(pieces)
    units, width = w.shape
    features = width // 2
    tokens = sum(p.shape[0] for p in pieces)
    first = acc is None
    return pl.pallas_call(
        functools.partial(grads_kernel, n, first, features, hidden_scale),
        in_specs=[HBM] * n + [VMEM] * (1 if first else 2),
        out_specs=VMEM,
        out_shape=pltpu.VMEM((units, width), F32),
        scratch_shapes=[
            pltpu.VMEM((tokens, width), BF16),
            pltpu.VMEM((units, tokens), BF16),
            pltpu.VMEM((units, tokens), BF16),
            pltpu.SemaphoreType.DMA((n,)),
        ],
        input_output_aliases={} if first else {n + 1: 0},
        compiler_params=pltpu.CompilerParams(vmem_limit_bytes=LIMIT),
        cost_estimate=pl.CostEstimate(
            flops=8 * tokens * units * features,
            bytes_accessed=tokens * width * 2,
            transcendentals=units * tokens,
        ),
        name="grads",
    )(*pieces, w, *(() if first else (acc,)))


def adam(total, scale, first, second, start):
    corr_one = 1.0 - BETA_ONE**STEP
    corr_two = 1.0 - BETA_TWO**STEP
    raw = total * scale
    first_new = (INNER_RATE * BETA_ONE / corr_one) * first.astype(F32) + (
        INNER_RATE * (1.0 - BETA_ONE) / corr_one
    ) * raw
    second_new = (BETA_TWO / corr_two) * second.astype(F32) + (
        (1.0 - BETA_TWO) / corr_two
    ) * (raw * raw)
    root = second_new * lax.rsqrt(second_new)
    return (first_new / (root + ADAM_EPS) + (INNER_RATE * DECAY) * start.astype(F32)).astype(BF16)


TAIL = (((2, 0), (2, 1)), ((0, 1), (1, 1), (3, 1)), ((0, 0), (1, 0), (3, 0)))


def pseudo_kernel(n, part, features, hidden_scale, *refs):
    where = refs[0]
    if part == 0:
        pieces = refs[1 : 1 + n]
        w, acc, m, v, out, xg, act_t, dpre_t, total, lines, sem = refs[1 + n :]
        fetch(pieces, xg, sem)
        hidden_both(xg, w, act_t, dpre_t, features, hidden_scale)
    else:
        w, acc, m, v, xg, act_t, dpre_t, out, total, lines = refs[1:]
    y, core = where[0], where[1]
    rows = w.shape[0] // SETS
    starts = []
    for d, other in TAIL[part]:
        parity = 1 - core if other else core
        chip = lax.rem(y + jnp.where(parity == 0, d, YS - d), YS)
        starts.append(pl.multiple_of((2 * chip + parity) * rows, rows))
    for half, left, scale in ((0, dpre_t, features ** (-0.5)), (1, act_t, hidden_scale)):
        for k, at in enumerate(starts):
            lines[k * rows : (k + 1) * rows, :] = left[pl.ds(at, rows), :]

        def columns(j, carry, half=half, scale=scale):
            cols = pl.ds(pl.multiple_of(half * features + j * COLS, COLS), COLS)
            total[...] = jnp.dot(lines[...], xg[:, cols], preferred_element_type=F32)
            for k, start in enumerate(starts):
                at = pl.ds(start, rows)
                grads = acc[at, cols] + total[k * rows : (k + 1) * rows, :]
                out[k, :, cols] = adam(grads, scale, m[at, cols], v[at, cols], w[at, cols])
            return carry

        lax.fori_loop(0, features // COLS, columns, 0)


def tail_pseudo(part, where, given, w, acc, m, v, hidden_scale):
    units, width = w.shape
    features = width // 2
    rows = units // SETS
    count = len(TAIL[part])
    tokens = sum(p.shape[0] for p in given) if part == 0 else given[0].shape[0]
    hid = pltpu.VMEM((units, tokens), BF16)
    kept = (w, acc, m, v)
    out_shape = [pltpu.VMEM((count, rows, width), BF16)]
    scratch = [pltpu.VMEM((count * rows, COLS), F32), pltpu.VMEM((count * rows, tokens), BF16)]
    if part == 0:
        operands, specs = (*given, *kept), [ANY] * len(given) + [VMEM] * 4
        out_shape += [pltpu.VMEM((tokens, width), BF16), hid, hid]
        scratch.append(pltpu.SemaphoreType.DMA((len(given),)))
    else:
        operands, specs = (*kept, *given), [VMEM] * 7
    return pl.pallas_call(
        functools.partial(pseudo_kernel, len(given), part, features, hidden_scale),
        in_specs=[pl.BlockSpec(memory_space=pltpu.SMEM)] + specs,
        out_specs=[VMEM] * len(out_shape),
        scratch_shapes=scratch,
        out_shape=out_shape,
        compiler_params=pltpu.CompilerParams(vmem_limit_bytes=LIMIT),
        cost_estimate=pl.CostEstimate(
            flops=4 * features * tokens * (rows * count + (units if part == 0 else 0)),
            bytes_accessed=rows * count * width * 12,
            transcendentals=rows * count * width,
        ),
        name="tail_%d" % part,
    )(where, *operands)


def home(info, d, parity):
    return 2 * lax.rem(info[0] + jnp.where(parity == 0, d, YS - d), YS) + parity


def run_copies(pairs, sem):
    copies = [pltpu.make_async_copy(a, b, sem.at[k]) for k, (a, b) in enumerate(pairs)]
    for c in copies:
        c.start()
    for c in copies:
        c.wait()


def near_own_kernel(info, own, nxt, prv, out, sem):
    run_copies(
        [(a.at[info[2 + d]], out.at[home(info, d, info[1])]) for a, d in ((own, 0), (nxt, 1), (prv, 3))],
        sem,
    )


def rest_kernel(info, near_own, near, own_l, own_r, other_l, other_r, begun, out, sem):
    half = own_l.shape[1]
    left, right = pl.ds(0, half), pl.ds(half, half)
    pairs = [
        (a, out.at[home(info, d, 1 - info[1])])
        for a, d in ((near_own, 0), (near.at[0], 1), (near.at[1], 3))
    ]
    for parity, l, r in ((info[1], own_l, own_r), (1 - info[1], other_l, other_r)):
        far = home(info, 2, parity)
        pairs += [(l, out.at[far, :, left]), (r, out.at[far, :, right])]
    run_copies(pairs, sem)


def assemble(kernel, info, pieces, begun, copies, rows, width):
    return pl.pallas_call(
        kernel,
        in_specs=[pl.BlockSpec(memory_space=pltpu.SMEM)]
        + [VMEM] * len(pieces)
        + [HBM] * len(begun),
        out_specs=HBM,
        out_shape=jax.ShapeDtypeStruct((SETS, rows, width), BF16),
        scratch_shapes=[pltpu.SemaphoreType.DMA((copies,))],
        input_output_aliases={1 + len(pieces): 0} if begun else {},
        compiler_params=pltpu.CompilerParams(vmem_limit_bytes=8 << 20),
        cost_estimate=pl.CostEstimate(
            flops=0, bytes_accessed=SETS * rows * width * 2, transcendentals=0
        ),
        name=kernel.__name__,
    )(info, *pieces, *begun)


def per_device(
    input_activation_matrix,
    output_sensitivity,
    trajectory_initial_parameters,
    trajectory_gradient_average,
    trajectory_squared_average,
    common_expert_parameters,
    outer_inertia,
    trajectory_membership,
    punctual_flags,
):
    set_count, rows, width = trajectory_initial_parameters.shape[1:]
    units = set_count * rows
    features = width // 2
    hidden_scale = (SETS * UNIT) ** (-0.5)
    w = trajectory_initial_parameters[0].reshape(units, width)
    m = trajectory_gradient_average[0].reshape(units, width)
    v = trajectory_squared_average[0].reshape(units, width)

    me = lax.axis_index("path")
    y, core = me // 2, me % 2
    choices = common_expert_parameters.shape[1]
    eligible = jnp.arange(choices, dtype=jnp.int32)
    chosen = jnp.where(
        (trajectory_membership[:, :, None] == eligible[None, None, :])
        & (punctual_flags[:, None, None] == 1),
        1.0,
        0.0,
    ).astype(F32)
    turn = 1 - 2 * core
    chips = (y + turn * jnp.arange(YS, dtype=jnp.int32)) % YS
    sets = 2 * chips + core
    nxt_chip, prv_chip = chips[1], chips[3]
    mate = me ^ 1
    paths = jnp.stack(
        [me] * 4
        + [mate] * 4
        + [2 * prv_chip + core, 2 * prv_chip + 1 - core]
        + [2 * nxt_chip + core, 2 * nxt_chip + 1 - core]
    )
    at_sets = jnp.concatenate([sets, sets, sets[1:2], sets[1:2], sets[3:], sets[3:]])
    weights = chosen[paths, at_sets]
    pick_paths = jnp.concatenate([paths[:8], paths[10:], paths[8:10]])
    pick_sets = jnp.concatenate([sets, sets, sets[3:], sets[3:], sets[1:2], sets[1:2]])
    picks = trajectory_membership[pick_paths, pick_sets]
    tally = jnp.sum(chosen[:, me], axis=0)
    share = jnp.maximum(tally, 1.0)[:, None, None]
    where = jnp.stack([y, core]).astype(jnp.int32)
    info = jnp.concatenate([where, picks[:4]]).astype(jnp.int32)

    calls = (
        ((0, 0), (0, -1), (0, 1), (0, 2)),
        ((-1, 0), (1, 0), (-1, -1), (1, -1)),
        ((-1, 1), (1, 1), (-1, 2), (1, 2)),
        ((2, 0), (2, 1)),
    )
    seconds = {k: picks[k] == 1 for k in (4, 5, 7, 8, 9, 10, 11)}
    w, where, weights, seconds, share, info = lax.optimization_barrier(
        (w, where, weights, seconds, share, info)
    )
    w, m, v = resident(w), resident(m), resident(v)
    acc = None

    def compute(k, got):
        nonlocal acc
        acc = accumulate([got[b] for b in calls[k]], w, acc, hidden_scale)
        return acc

    got = gather_tokens(input_activation_matrix[0], output_sensitivity[0], compute)
    rest = [got[2, -1], got[2, 2]]

    common = common_expert_parameters[0]
    inertia = outer_inertia[0]

    def weighed(k, a):
        return weights[k][:, None, None] * a.astype(F32)[None]

    acc = resident(acc)
    far, *given = tail_pseudo(0, where, rest, w, acc, m, v, hidden_scale)
    given = [resident(a) for a in given]
    l_same, r_same = on_path(far[0, :, :features], 1), on_path(far[0, :, features:], -1)
    l_cross, r_cross = on_path(far[1, :, :features], -1, 1), on_path(far[1, :, features:], 1, 1)
    (swap,) = tail_pseudo(1, where, given, w, acc, m, v, hidden_scale)
    mate_keep = on_path(after(swap, l_same, r_same), 0, 1)
    (keep,) = tail_pseudo(2, after(where, swap), given, w, acc, m, v, hidden_scale)

    def merged(i, d, lo=0, hi=width):
        return weighed(d, keep[i, :, lo:hi]) + weighed(4 + d, mate_keep[i, :, lo:hi])

    up_l = merged(1, 1, 0, features) + weighed(8, l_same) + weighed(9, l_cross)
    down_r = merged(2, 3, features) + weighed(10, r_same) + weighed(11, r_cross)
    up = jnp.concatenate([up_l.astype(BF16), merged(1, 1, features).astype(BF16)], -1)
    down = jnp.concatenate([merged(2, 3, 0, features).astype(BF16), down_r.astype(BF16)], -1)
    part_up, part_down = on_path(up, 1), on_path(down, -1)
    total = merged(0, 0) + part_up.astype(F32) + part_down.astype(F32)

    def refreshed(total):
        average = total / share
        new_inertia = INERTIA_FACTOR * inertia + average
        return common - GLOBAL_LEARNING * (average + INERTIA_FACTOR * new_inertia), new_inertia

    updated = refreshed(total)[0].astype(BF16)
    prv, nxt = on_path(updated, 1), on_path(updated, -1)
    new_experts, new_inertia = refreshed(after(total, prv, nxt))

    def picked(k, a, lo=0, hi=width):
        return jnp.where(seconds[k], a[1, :, lo:hi], a[0, :, lo:hi])

    own_l = on_path(picked(8, prv, 0, features), 1)
    other_l = on_path(picked(9, prv, 0, features), 1, 1)
    own_r = on_path(picked(10, nxt, features), -1)
    other_r = on_path(picked(11, nxt, features), -1, 1)
    near_own = on_path(picked(4, updated), 0, 1)
    near = on_path(jnp.stack([picked(5, nxt), picked(7, prv)]), 0, 1)
    returned = assemble(near_own_kernel, info, [resident(a) for a in (updated, nxt, prv)], (), 3, rows, width)
    sent = [resident(a) for a in (near_own, near, own_l, own_r, other_l, other_r)]
    returned = assemble(rest_kernel, info, sent, (returned,), 7, rows, width)
    return (new_experts[None], new_inertia[None], returned[None])


def solution(mesh):
    placed = (
        P("path", "fsdp", None),
        P("path", "fsdp", None),
        P("path", None, "fsdp", None),
        P("path", None, "fsdp", None),
        P("path", None, "fsdp", None),
        P("path", None, "fsdp", None),
        P("path", None, "fsdp", None),
        P(),
        P(),
    )
    return jax.shard_map(
        per_device,
        mesh=mesh,
        in_specs=placed,
        out_specs=(
            P("path", None, "fsdp", None),
            P("path", None, "fsdp", None),
            P("path", None, "fsdp", None),
        ),
        check_vma=False,
    )
```
